128 devices in a mesh: gx: 16 (over z, y), gy: 8 (over x, core).
Axes of the slice: x: 4, y: 4, z: 4, core: 2. Of those that a mesh axis runs over, the one named last changes fastest.
Arguments:
- object_field: float32 [2, 4096, 8192], P(None, 'gy', 'gx'), may hold values from -6 to 6
- probe: float32 [2, 256, 256], replicated, may hold values from -4 to 4
- frames: float32 [8, 16, 16, 2, 256, 256], P('gy', 'gx'), may hold values from 0.2 to 5
- positions: int32 [8, 16, 24, 2], P('gy', 'gx'), may hold values from -128 to 384
- helpers: int32 [8, 16, 24, 1], P('gy', 'gx'), may hold values from 0 to 15; in each aligned block of 24 rows (0 to 23, 24 to 47, ..., all dimensions but the last counted through in order) at most 2 rows name the same one
- task_counts: int32 [8, 16], P('gy', 'gx'), may hold values from 6 to 24, as said below
Outputs:
- updated_field: float32 [2, 4096, 8192], P(None, 'gy', 'gx')
The draws below stay inside these ranges and needn't reach their ends.
Inputs may be any that keep to these rules, and one draw needn't show every extreme that they name: `helpers`: among one tile's 24 task slots no helper column is named more than 2 times, and in some tiles one is named exactly 2 times. `task_counts`: some tile has all 24 tasks valid.
All inputs are finite; a program needn't handle non-finite values.
Results may differ from the reference program's by a relative error of at most 0.0003.
Values sent between devices are 32-bit elements; how exact they have to be, the bound alone decides.
No kernel may reach another device: no remote copies, remote signals or barrier semaphores. Data moves between devices by JAX's collectives and lax.ppermute only.
A program may use at most 192 MiB of HBM per device.

```python
import math
import jax
import jax.numpy as jnp
import numpy as np
from jax import lax

TILE = 512
PATCH = 256
TASKS = 24
TROWS = 8
TCOLS = 16
SLOT = 2
NROWS = 4096
NCOLS = 8192


def draw_task_counts(key, part):
    first_key, second_key = jax.random.split(jax.random.fold_in(key, 71))
    counted = jax.random.randint(first_key, (TROWS * TCOLS,), TASKS // 4, TASKS + 1)
    chosen = jax.random.randint(second_key, (), 0, TROWS * TCOLS)
    filled = jnp.where(jnp.arange(TROWS * TCOLS) == chosen, TASKS, counted)
    return filled.reshape(TROWS, TCOLS).astype(jnp.int32)


def set_ends(drawn, stream_key, least, largest):
    dims = drawn.shape
    spot = [jax.random.randint(jax.random.fold_in(stream_key, axis), (), 0, dims[axis]) for axis in range(len(dims))]
    drawn = drawn.at[tuple(spot)].set(least)
    longest = dims.index(max(dims))
    spot[longest] = (spot[longest] + 1) % dims[longest]
    return drawn.at[tuple(spot)].set(largest)


def shard_levels(rng, extent, cuts, least, largest):
    def one(position, parts):
        draws = jax.random.uniform(jax.random.fold_in(jax.random.fold_in(rng, 6), position), (parts,), jnp.float32, least / len(cuts), largest / len(cuts))
        return jnp.repeat(jnp.exp(draws), extent[position] // parts).reshape((-1,) + (1,) * (len(extent) - position - 1))

    loudness = one(*cuts[0])
    for cut in cuts[1:]:
        loudness = loudness * one(*cut)
    return loudness


def shared_out(stream_key, own, number, rows, amount, top, bound, lean):
    ranking = jax.random.permutation(stream_key, amount)
    heavy_load, common = load_shares(amount, rows * top, bound, lean, True), load_shares(amount, rows * top, bound, lean, False)
    places = jnp.arange(amount)

    def named(tallies, offset_by):
        used = int((tallies > 0).sum())
        fixed = max(1, used // 4)
        passed = fixed + (places - fixed + offset_by * (used - fixed)) % max(1, amount - fixed)
        return jnp.zeros((amount,), jnp.int32).at[ranking[jnp.where(places < fixed, places, passed)]].set(jnp.asarray(tallies, jnp.int32))

    tallies = jnp.where(number % 4 == 0, named(heavy_load, number // 4), named(common, number - number // 4 - 1))
    mixed = jax.random.permutation(jax.random.fold_in(own, 3), amount)
    donor, receiver = mixed[0:amount // 2 * 2:2], mixed[1:amount // 2 * 2:2]
    slack = jnp.minimum(tallies[donor] - 1, bound - tallies[receiver]) // 2
    slack = jnp.where((donor == ranking[0]) | (receiver == ranking[0]) | (tallies[receiver] == 0), 0, jnp.maximum(slack, 0))
    passed = jax.random.randint(jax.random.fold_in(own, 4), (amount // 2,), 0, 1 << 20) % (slack + 1)
    tallies = tallies.at[donor].add(-passed).at[receiver].add(passed)
    labels = jnp.searchsorted(jnp.cumsum(tallies), jnp.arange(rows * top), side="right").astype(jnp.int32)
    grid = labels.reshape(top, rows).T
    grid = grid[jax.random.permutation(jax.random.fold_in(own, 1), rows)]
    offset_by = jax.random.randint(jax.random.fold_in(own, 2), (rows, 1), 0, top)
    return jnp.take_along_axis(grid, (jnp.arange(top)[None, :] + offset_by) % top, axis=1)


def load_shares(number_of, total, most, slope, full):
    weights = [(1 << 20) // math.isqrt(rank ** slope) + 1 for rank in range(1, number_of + 1)]
    largest = most if full else min(most, max(-(-total // number_of), total * weights[0] // sum(weights)))
    least = 1 if total - largest >= number_of - 1 else 0
    given, spare = [largest] + [least] * (number_of - 1), total - largest - least * (number_of - 1)
    while spare > 0:
        free = [i for i in range(1, number_of) if given[i] < largest] or [i for i in range(1, number_of) if given[i] < most]
        mass, left = sum([weights[i] for i in free]), spare
        for i in free:
            addition = min(most - given[i], max(1, left * weights[i] // mass), spare)
            given[i] = given[i] + addition
            spare = spare - addition
    return np.array(given)


def centred(own_key, extent, width, reach, cuts=(), kind=jnp.bfloat16):
    values = jax.random.normal(own_key, extent, jnp.float32) * width
    if len(cuts) > 0:
        values = shard_levels(own_key, extent, cuts, -0.22, 0.18) * values
    return jnp.clip(values, min=-reach, max=reach).astype(kind)


def setup_inputs(seed: int = 0) -> dict:
    splits = jax.random.split(jax.random.key(seed), 7)
    object_field = centred(splits[0], (2, NROWS, NCOLS), 1.0, 6.0, ((1, 8), (2, 16)), jnp.float32)
    probe = centred(splits[1], (2, PATCH, PATCH), 0.7, 4.0, (), jnp.float32)
    frames = jnp.clip(jnp.exp(math.log(5.0) - 3.218876 * jax.random.uniform(splits[2], (TROWS, TCOLS, TCOLS, SLOT, PATCH, PATCH), jnp.float32) ** shard_levels(splits[2], (TROWS, TCOLS, TCOLS, SLOT, PATCH, PATCH), ((0, 8), (1, 16)), -0.2, 0.2)), 0.2, 5.0)
    positions = set_ends(jax.random.randint(splits[3], (TROWS, TCOLS, TASKS, 2), 0 - PATCH // 2, TILE - PATCH // 2 + 1), jax.random.fold_in(splits[3], 1), 0 - PATCH // 2, (TILE - PATCH // 2 + 1) - 1).astype(jnp.int32)
    helpers_keys = jax.random.split(jax.random.fold_in(splits[4], 1), TROWS * TCOLS * TASKS // TASKS)
    helpers_turns = jax.random.permutation(jax.random.fold_in(splits[4], 3), TROWS * TCOLS * TASKS // TASKS)
    helpers = jax.vmap(lambda own, number: shared_out(jax.random.fold_in(splits[4], 2), own, number, TASKS, TCOLS, 1, SLOT, 2))(helpers_keys, helpers_turns).reshape((TROWS, TCOLS, TASKS, 1))
    task_counts = draw_task_counts(jax.random.fold_in(splits[6], 71), 0)
    return {"object_field": object_field, "probe": probe, "frames": frames, "positions": positions, "helpers": helpers, "task_counts": task_counts}


step_size = 0.1
ridge = 0.5

def dft_tables(length):
    index = jnp.arange(length, dtype=jnp.int32)
    phase = index[:, None] * index[None, :] % length
    angle = 2.0 * jnp.pi / length * phase.astype(jnp.float32)
    factor = length ** (-0.5)
    return (jnp.cos(angle) * factor, -jnp.sin(angle) * factor)

def right_mul(real_in, imag_in, table_re, table_im):
    highest = lax.Precision.HIGHEST
    first = jnp.einsum('bij,jk->bik', real_in, table_re, precision=highest)
    second = jnp.einsum('bij,jk->bik', imag_in, table_im, precision=highest)
    third = jnp.einsum('bij,jk->bik', real_in + imag_in, table_re + table_im, precision=highest)
    return (first - second, third - first - second)

def left_mul(table_re, table_im, real_in, imag_in):
    highest = lax.Precision.HIGHEST
    first = jnp.einsum('ij,bjk->bik', table_re, real_in, precision=highest)
    second = jnp.einsum('ij,bjk->bik', table_im, imag_in, precision=highest)
    third = jnp.einsum('ij,bjk->bik', table_re + table_im, real_in + imag_in, precision=highest)
    return (first - second, third - first - second)

def transform(real_in, imag_in, table_re, table_im):
    mid_re, mid_im = right_mul(real_in, imag_in, table_re, table_im)
    return left_mul(table_re, table_im, mid_re, mid_im)

def task_grad(patches, measured, probe):
    length = patches.shape[-1]
    table_re, table_im = dft_tables(length)
    table_re = table_re.astype(patches.dtype)
    table_im = table_im.astype(patches.dtype)
    probe_re, probe_im = (probe[0], probe[1])
    obj_re, obj_im = (patches[:, 0], patches[:, 1])
    wave_re = probe_re * obj_re - probe_im * obj_im
    wave_im = probe_re * obj_im + probe_im * obj_re
    far_re, far_im = transform(wave_re, wave_im, table_re, table_im)
    weight = far_re * far_re + far_im * far_im - measured
    back_re, back_im = transform(weight * far_re, weight * far_im, table_re, -table_im)
    grad_re = probe_re * back_re + probe_im * back_im
    grad_im = probe_re * back_im - probe_im * back_re
    return jnp.stack([grad_re, grad_im], axis=1)

def reference(object_field, probe, frames, positions, helpers, task_counts):
    half = PATCH // 2
    padded = jnp.pad(object_field, ((0, 0), (half, half), (half, half)))
    task_ids = jnp.arange(TASKS, dtype=jnp.int32)
    helper_cols = helpers[..., 0].astype(jnp.int32)
    same = helper_cols[..., :, None] == helper_cols[..., None, :]
    earlier = task_ids[None, :] < task_ids[:, None]
    ranks = lax.optimization_barrier(jnp.sum(jnp.logical_and(same, earlier), axis=-1)).astype(jnp.int32)
    valid = task_ids < task_counts[..., None]
    row_ids = jnp.broadcast_to(jnp.arange(TROWS, dtype=jnp.int32)[:, None, None], (TROWS, TCOLS, TASKS))
    col_ids = jnp.broadcast_to(jnp.arange(TCOLS, dtype=jnp.int32)[None, :, None], (TROWS, TCOLS, TASKS))
    listing = (row_ids.reshape(-1), col_ids.reshape(-1), positions[..., 0].astype(jnp.int32).reshape(-1), positions[..., 1].astype(jnp.int32).reshape(-1), helper_cols.reshape(-1), ranks.reshape(-1), valid.reshape(-1))
    zero = jnp.int32(0)

    def one_task(grad, item):
        row, col, off_y, off_x, helper, rank, live = item
        start_y = (row * TILE + off_y + half).astype(jnp.int32)
        start_x = (col * TILE + off_x + half).astype(jnp.int32)
        patch = lax.dynamic_slice(padded, (zero, start_y, start_x), (2, PATCH, PATCH))
        patch = patch * live.astype(padded.dtype)
        measured = frames[row, helper, col, rank]
        piece = task_grad(patch[None], measured[None], probe)[0]
        current = lax.dynamic_slice(grad, (zero, start_y, start_x), (2, PATCH, PATCH))
        return (lax.dynamic_update_slice(grad, current + piece, (zero, start_y, start_x)), None)
    grad, unused = lax.scan(one_task, jnp.zeros_like(padded), listing)
    gradient = grad[:, half:half + NROWS, half:half + NCOLS]
    return object_field - step_size * (gradient + ridge * object_field)
```

```python
import functools

import jax
import jax.numpy as jnp
import ml_dtypes
import numpy as np
from jax import lax
from jax.experimental import pallas as pl
from jax.experimental.pallas import tpu as pltpu
from jax.sharding import PartitionSpec as P

PATCH = 256
HALF = 128
TASKS = 24
BLOCKS = 3
EXT = 768

step_size = 0.1
ridge = 0.5

f32 = jnp.float32
bf16 = jnp.bfloat16


def tables():
    j = np.arange(HALF)
    even = np.exp(-2j * np.pi * (np.outer(j, 2 * j) % PATCH) / PATCH) / 16.0
    odd = np.exp(-2j * np.pi * (np.outer(j, 2 * j + 1) % PATCH) / PATCH) / 16.0

    def left(w):
        return np.block([[w.real, -w.imag], [w.imag, w.real]])

    def split(w):
        high = w.astype(ml_dtypes.bfloat16)
        low = (w - high.astype(np.float64)).astype(ml_dtypes.bfloat16)
        return high, low

    pairs = [split(left(w)) for w in (even, odd)]
    lefts = np.stack([np.stack(pair) for pair in pairs])
    return jnp.asarray(lefts), jnp.asarray(np.swapaxes(lefts, 2, 3).copy())


def shuffle():
    p = np.zeros((PATCH, PATCH), np.float32)
    j = np.arange(HALF)
    p[2 * j, j] = 1
    p[2 * j + 1, HALF + j] = 1
    return p.astype(ml_dtypes.bfloat16)


def two_terms(x):
    high = x.astype(bf16)
    low = (x - high.astype(f32)).astype(bf16)
    return high, low


def right_dot(x, w):
    high, low = two_terms(x)
    both = jnp.concatenate([high, low, high], axis=1)
    return jnp.dot(both, jnp.concatenate([w[0], w[0], w[1]], axis=0), preferred_element_type=f32)


def left_dot(w, x):
    high, low = two_terms(x)
    both = jnp.concatenate([high, low, high], axis=0)
    return jnp.dot(jnp.concatenate([w[0], w[0], w[1]], axis=1), both, preferred_element_type=f32)


def three_dot(x, p):
    high = x.astype(bf16)
    rest = x - high.astype(f32)
    mid = rest.astype(bf16)
    low = (rest - mid.astype(f32)).astype(bf16)
    out = jnp.dot(high, p, preferred_element_type=f32)
    out = out + jnp.dot(mid, p, preferred_element_type=f32)
    return out + jnp.dot(low, p, preferred_element_type=f32)


def prep_kernel(ext_ref, perm_ref, out_ref, even_ref, odd_ref):
    rows = ext_ref.shape[1]
    for c in range(2):
        for b in range(ext_ref.shape[2] // PATCH):
            mixed = three_dot(ext_ref[c, :, b * PATCH : (b + 1) * PATCH], perm_ref[...])
            even_ref[...] = mixed[:, :HALF]
            odd_ref[...] = mixed[:, HALF:]
            for q in range(2):
                out_ref[c, 0, b, q] = even_ref[pl.ds(q, rows // 2, stride=2), :]
                out_ref[c, 1, b, q] = odd_ref[pl.ds(q, rows // 2, stride=2), :]


def prep(ext):
    rows, cols = ext.shape[1:]
    return pl.pallas_call(
        prep_kernel,
        out_shape=jax.ShapeDtypeStruct((2, 2, cols // PATCH, 2, rows // 2, HALF), f32),
        in_specs=[pl.BlockSpec(memory_space=pltpu.VMEM)] * 2,
        out_specs=pl.BlockSpec(memory_space=pltpu.VMEM),
        scratch_shapes=[pltpu.VMEM((rows, HALF), f32)] * 2,
        compiler_params=pltpu.CompilerParams(vmem_limit_bytes=40 << 20),
        cost_estimate=pl.CostEstimate(flops=6 * rows * cols * PATCH * 2, bytes_accessed=16 * rows * cols, transcendentals=0),
    )(ext, jnp.asarray(shuffle()))


def window(pos_ref, t):
    start_y = pos_ref[2 * t] + HALF
    start_x = pos_ref[2 * t + 1] + HALF
    block = jnp.where(start_x >= PATCH, 1, 0)
    offset = start_x - block * PATCH
    rows = [((start_y + q) & 1, (start_y + q) >> 1) for q in range(2)]
    return block, offset, rows


def rolled_probe(probe_ref, offset, p, q):
    source = (p + offset) & 1
    amount = ((offset + source - p) >> 1) & (HALF - 1)
    return [pltpu.roll(probe_ref[c, source, 0, q], amount, 1) for c in range(2)]


def lane_mask(offset, p):
    lane = lax.broadcasted_iota(jnp.int32, (HALF, HALF), 1)
    return lane >= ((offset + 1 - p) >> 1)


def forward_kernel(pos_ref, count_ref, obj_ref, probe_ref, left_ref, right_ref, out_ref):
    t = pl.program_id(0)

    @pl.when(t < count_ref[0])
    def _():
        block, offset, rows = window(pos_ref, t)
        parts = []
        for p in range(2):
            mask = lane_mask(offset, p)
            waves = []
            for q in range(2):
                parity, first = rows[q]
                o = [
                    jnp.where(
                        mask,
                        obj_ref[c, p, block, parity, pl.ds(first, HALF), :],
                        obj_ref[c, p, block + 1, parity, pl.ds(first, HALF), :],
                    )
                    for c in range(2)
                ]
                w = rolled_probe(probe_ref, offset, p, q)
                waves.append(jnp.concatenate([w[0] * o[0] - w[1] * o[1], w[0] * o[1] + w[1] * o[0]], axis=1))
            parts.append(right_dot(jnp.concatenate(waves, axis=0), right_ref[p]))
        low = parts[0] + parts[1]
        high = parts[0] - parts[1]
        sides = []
        for q in range(2):
            r = slice(q * HALF, (q + 1) * HALF)
            re = jnp.concatenate([low[r, :HALF], high[r, :HALF]], axis=1)
            im = jnp.concatenate([low[r, HALF:], high[r, HALF:]], axis=1)
            sides.append(left_dot(left_ref[q], jnp.concatenate([re, im], axis=0)))
        out_ref[0, 0] = sides[0] + sides[1]
        out_ref[0, 1] = sides[0] - sides[1]


def forward(pos, count, obj, probe, lefts, rights):
    whole = pl.BlockSpec(memory_space=pltpu.VMEM)
    return pl.pallas_call(
        forward_kernel,
        out_shape=jax.ShapeDtypeStruct((TASKS, 2, PATCH, PATCH), f32),
        grid_spec=pltpu.PrefetchScalarGridSpec(
            num_scalar_prefetch=2,
            grid=(TASKS,),
            in_specs=[whole] * 4,
            out_specs=pl.BlockSpec((1, 2, PATCH, PATCH), lambda t, pos, count: (t, 0, 0, 0)),
        ),
        compiler_params=pltpu.CompilerParams(vmem_limit_bytes=40 << 20),
        cost_estimate=pl.CostEstimate(flops=TASKS * 24 * PATCH**3, bytes_accessed=TASKS * 8 * PATCH**2, transcendentals=0),
    )(pos, count, obj, probe, lefts, rights)


def inverse_kernel(pos_ref, slot_ref, count_ref, far_ref, frame_ref, probe_ref, left_ref, right_ref, perm_ref, out_ref, acc_ref, even_ref, odd_ref):
    t = pl.program_id(0)

    @pl.when(t == 0)
    def _():
        acc_ref[...] = jnp.zeros_like(acc_ref)

    @pl.when(t < count_ref[0])
    def _():
        block, offset, rows = window(pos_ref, t)
        weighted = []
        for h in range(2):
            re = far_ref[0, h, :HALF, :]
            im = far_ref[0, h, HALF:, :]
            weight = re * re + im * im - frame_ref[0, h * HALF : (h + 1) * HALF, :]
            weighted.append(jnp.concatenate([weight * re, weight * im], axis=0))
        back = [
            left_dot(right_ref[0], weighted[0] + weighted[1]),
            left_dot(right_ref[1], weighted[0] - weighted[1]),
        ]
        low = [jnp.concatenate([b[:HALF, :HALF], b[HALF:, :HALF]], axis=1) for b in back]
        high = [jnp.concatenate([b[:HALF, HALF:], b[HALF:, HALF:]], axis=1) for b in back]
        low = jnp.concatenate(low, axis=0)
        high = jnp.concatenate(high, axis=0)
        chis = [right_dot(low + high, left_ref[0]), right_dot(low - high, left_ref[1])]
        for p in range(2):
            mask = lane_mask(offset, p)
            for q in range(2):
                parity, first = rows[q]
                w = rolled_probe(probe_ref, offset, p, q)
                re = chis[p][q * HALF : (q + 1) * HALF, :HALF]
                im = chis[p][q * HALF : (q + 1) * HALF, HALF:]
                g = [w[0] * re + w[1] * im, w[0] * im - w[1] * re]
                for c in range(2):
                    here = (c, p, block, parity, pl.ds(first, HALF), slice(None))
                    acc_ref[here] = acc_ref[here] + jnp.where(mask, g[c], 0.0)
                    there = (c, p, block + 1, parity, pl.ds(first, HALF), slice(None))
                    acc_ref[there] = acc_ref[there] + jnp.where(mask, 0.0, g[c])

    @pl.when(t == TASKS - 1)
    def _():
        for c in range(2):
            for b in range(BLOCKS):
                for q in range(2):
                    even_ref[pl.ds(q, EXT // 2, stride=2), :] = acc_ref[c, 0, b, q]
                    odd_ref[pl.ds(q, EXT // 2, stride=2), :] = acc_ref[c, 1, b, q]
                mixed = jnp.concatenate([even_ref[...], odd_ref[...]], axis=1)
                out_ref[c, :, b * PATCH : (b + 1) * PATCH] = three_dot(mixed, perm_ref[...])


def inverse(pos, slot, count, far, frames, probe, lefts, rights):
    whole = pl.BlockSpec(memory_space=pltpu.VMEM)
    return pl.pallas_call(
        inverse_kernel,
        out_shape=jax.ShapeDtypeStruct((2, EXT, EXT), f32),
        grid_spec=pltpu.PrefetchScalarGridSpec(
            num_scalar_prefetch=3,
            grid=(TASKS,),
            in_specs=[
                pl.BlockSpec((1, 2, PATCH, PATCH), lambda t, pos, slot, count: (t, 0, 0, 0)),
                pl.BlockSpec((1, PATCH, PATCH), lambda t, pos, slot, count: (slot[t], 0, 0)),
                whole,
                whole,
                whole,
                whole,
            ],
            out_specs=whole,
            scratch_shapes=[
                pltpu.VMEM((2, 2, BLOCKS, 2, EXT // 2, HALF), f32),
                pltpu.VMEM((EXT, HALF), f32),
                pltpu.VMEM((EXT, HALF), f32),
            ],
        ),
        compiler_params=pltpu.CompilerParams(vmem_limit_bytes=40 << 20),
        cost_estimate=pl.CostEstimate(flops=TASKS * 24 * PATCH**3, bytes_accessed=TASKS * 12 * PATCH**2, transcendentals=0),
    )(pos, slot, count, far, frames, probe, lefts, rights, jnp.asarray(shuffle().T.copy()))


def extended_2(block, sides, width):
    for axis, dim in sides:
        count = lax.axis_size(axis)
        forward_pairs = [(i, i + 1) for i in range(count - 1)]
        backward_pairs = [(target, source) for source, target in forward_pairs]
        low = lax.ppermute(lax.slice_in_dim(block, block.shape[dim] - width, None, axis=dim), axis, forward_pairs)
        high = lax.ppermute(lax.slice_in_dim(block, 0, width, axis=dim), axis, backward_pairs)
        block = jnp.concatenate([low, block, high], axis=dim)
    return block


def exchanged(first, last, axis):
    count = lax.axis_size(axis)
    up = [(i, i + 1) for i in range(count - 1)]
    down = [(i + 1, i) for i in range(count - 1)]
    return lax.ppermute(last, axis, up), lax.ppermute(first, axis, down)


def local(extended, probe, arrived, offsets, helper_cols, count):
    task_ids = jnp.arange(TASKS, dtype=jnp.int32)
    same = helper_cols[:, None] == helper_cols[None, :]
    ranks = jnp.sum(jnp.logical_and(same, task_ids[None, :] < task_ids[:, None]), axis=1).astype(jnp.int32)
    slot = helper_cols * 2 + ranks
    lefts, rights = tables()
    obj = prep(extended)
    pro = prep(probe)
    far = forward(offsets, count, obj, pro, lefts, rights)
    return inverse(offsets, slot, count, far, arrived, pro, lefts, rights)


def per_device(object_field, probe, frames, positions, helpers, task_counts):
    arrived = lax.all_to_all(frames[0, 0], "gx", split_axis=0, concat_axis=0, tiled=True)
    extended = extended_2(object_field, (("gx", 2), ("gy", 1)), HALF)
    total = local(
        extended,
        probe,
        arrived.reshape(-1, PATCH, PATCH),
        positions[0, 0].reshape(-1),
        helpers[0, 0, :, 0],
        task_counts[0],
    )

    tile = object_field.shape[1]
    left_in, right_in = exchanged(total[:, :, :HALF], total[:, :, HALF + tile :], "gx")
    middle = total[:, :, HALF : HALF + tile]
    middle = middle.at[:, :, :HALF].add(left_in)
    middle = middle.at[:, :, tile - HALF :].add(right_in)
    up_in, down_in = exchanged(middle[:, :HALF, :], middle[:, HALF + tile :, :], "gy")
    gradient = middle[:, HALF : HALF + tile, :]
    gradient = gradient.at[:, :HALF, :].add(up_in)
    gradient = gradient.at[:, tile - HALF :, :].add(down_in)
    return object_field - step_size * (gradient + ridge * object_field)


def solution(mesh):
    in_specs = (
        P(None, "gy", "gx"),
        P(),
        P("gy", "gx", None, None, None, None),
        P("gy", "gx", None, None),
        P("gy", "gx", None, None),
        P("gy", "gx"),
    )
    out_specs = P(None, "gy", "gx")
    return jax.shard_map(per_device, mesh=mesh, in_specs=in_specs, out_specs=out_specs, check_vma=False)
```

```python
import functools

import jax
import jax.numpy as jnp
import ml_dtypes
import numpy as np
from jax import lax
from jax.experimental import pallas as pl
from jax.experimental.pallas import tpu as pltpu
from jax.sharding import PartitionSpec as P


PATCH = 256
HALF = 128
TASKS = 24
BLOCKS = 3
EXT = 768

step_size = 0.1
ridge = 0.5

f32 = jnp.float32
bf16 = jnp.bfloat16


def tables():
    j = np.arange(HALF)
    even = np.exp(-2j * np.pi * (np.outer(j, 2 * j) % PATCH) / PATCH) / 16.0
    odd = np.exp(-2j * np.pi * (np.outer(j, 2 * j + 1) % PATCH) / PATCH) / 16.0

    def left(w):
        return np.block([[w.real, -w.imag], [w.imag, w.real]])

    def split(w):
        high = w.astype(ml_dtypes.bfloat16)
        low = (w - high.astype(np.float64)).astype(ml_dtypes.bfloat16)
        return high, low

    pairs = [split(left(w)) for w in (even, odd)]
    lefts = np.stack([np.stack(pair) for pair in pairs])
    return jnp.asarray(lefts), jnp.asarray(np.swapaxes(lefts, 2, 3).copy())


def shuffle():
    p = np.zeros((PATCH, PATCH), np.float32)
    j = np.arange(HALF)
    p[2 * j, j] = 1
    p[2 * j + 1, HALF + j] = 1
    return p.astype(ml_dtypes.bfloat16)


def two_terms(x):
    high = x.astype(bf16)
    low = (x - high.astype(f32)).astype(bf16)
    return high, low


def right_dot(x, w):
    high, low = two_terms(x)
    both = jnp.concatenate([high, low, high], axis=1)
    return jnp.dot(both, jnp.concatenate([w[0], w[0], w[1]], axis=0), preferred_element_type=f32)


def left_dot(w, x):
    high, low = two_terms(x)
    both = jnp.concatenate([high, low, high], axis=0)
    return jnp.dot(jnp.concatenate([w[0], w[0], w[1]], axis=1), both, preferred_element_type=f32)


def three_dot(x, p):
    high = x.astype(bf16)
    rest = x - high.astype(f32)
    mid = rest.astype(bf16)
    low = (rest - mid.astype(f32)).astype(bf16)
    out = jnp.dot(high, p, preferred_element_type=f32)
    out = out + jnp.dot(mid, p, preferred_element_type=f32)
    return out + jnp.dot(low, p, preferred_element_type=f32)


def prep_kernel(ext_ref, perm_ref, out_ref, even_ref, odd_ref):
    rows = ext_ref.shape[1]
    for c in range(2):
        for b in range(ext_ref.shape[2] // PATCH):
            mixed = three_dot(ext_ref[c, :, b * PATCH : (b + 1) * PATCH], perm_ref[...])
            even_ref[...] = mixed[:, :HALF]
            odd_ref[...] = mixed[:, HALF:]
            for q in range(2):
                out_ref[c, 0, b, q] = even_ref[pl.ds(q, rows // 2, stride=2), :]
                out_ref[c, 1, b, q] = odd_ref[pl.ds(q, rows // 2, stride=2), :]


def prep(ext):
    rows, cols = ext.shape[1:]
    return pl.pallas_call(
        prep_kernel,
        out_shape=jax.ShapeDtypeStruct((2, 2, cols // PATCH, 2, rows // 2, HALF), f32),
        in_specs=[pl.BlockSpec(memory_space=pltpu.VMEM)] * 2,
        out_specs=pl.BlockSpec(memory_space=pltpu.VMEM),
        scratch_shapes=[pltpu.VMEM((rows, HALF), f32)] * 2,
        compiler_params=pltpu.CompilerParams(vmem_limit_bytes=40 << 20),
        cost_estimate=pl.CostEstimate(flops=6 * rows * cols * PATCH * 2, bytes_accessed=16 * rows * cols, transcendentals=0),
    )(ext, jnp.asarray(shuffle()))


def window(pos_ref, t):
    start_y = pos_ref[2 * t] + HALF
    start_x = pos_ref[2 * t + 1] + HALF
    block = jnp.where(start_x >= PATCH, 1, 0)
    offset = start_x - block * PATCH
    rows = [((start_y + q) & 1, (start_y + q) >> 1) for q in range(2)]
    return block, offset, rows


def rolled_probe(probe_ref, offset, p, q):
    source = (p + offset) & 1
    amount = ((offset + source - p) >> 1) & (HALF - 1)
    return [pltpu.roll(probe_ref[c, source, 0, q], amount, 1) for c in range(2)]


def lane_mask(offset, p):
    lane = lax.broadcasted_iota(jnp.int32, (HALF, HALF), 1)
    return lane >= ((offset + 1 - p) >> 1)


def forward_kernel(pos_ref, count_ref, obj_ref, probe_ref, left_ref, right_ref, out_ref):
    t = pl.program_id(0)

    @pl.when(t < count_ref[0])
    def _():
        block, offset, rows = window(pos_ref, t)
        parts = []
        for p in range(2):
            mask = lane_mask(offset, p)
            waves = []
            for q in range(2):
                parity, first = rows[q]
                o = [
                    jnp.where(
                        mask,
                        obj_ref[c, p, block, parity, pl.ds(first, HALF), :],
                        obj_ref[c, p, block + 1, parity, pl.ds(first, HALF), :],
                    )
                    for c in range(2)
                ]
                w = rolled_probe(probe_ref, offset, p, q)
                waves.append(jnp.concatenate([w[0] * o[0] - w[1] * o[1], w[0] * o[1] + w[1] * o[0]], axis=1))
            parts.append(right_dot(jnp.concatenate(waves, axis=0), right_ref[p]))
        low = parts[0] + parts[1]
        high = parts[0] - parts[1]
        sides = []
        for q in range(2):
            r = slice(q * HALF, (q + 1) * HALF)
            re = jnp.concatenate([low[r, :HALF], high[r, :HALF]], axis=1)
            im = jnp.concatenate([low[r, HALF:], high[r, HALF:]], axis=1)
            sides.append(left_dot(left_ref[q], jnp.concatenate([re, im], axis=0)))
        out_ref[0, 0] = sides[0] + sides[1]
        out_ref[0, 1] = sides[0] - sides[1]


def forward(pos, count, obj, probe, lefts, rights):
    whole = pl.BlockSpec(memory_space=pltpu.VMEM)
    return pl.pallas_call(
        forward_kernel,
        out_shape=jax.ShapeDtypeStruct((TASKS, 2, PATCH, PATCH), f32),
        grid_spec=pltpu.PrefetchScalarGridSpec(
            num_scalar_prefetch=2,
            grid=(TASKS,),
            in_specs=[whole] * 4,
            out_specs=pl.BlockSpec((1, 2, PATCH, PATCH), lambda t, pos, count: (t, 0, 0, 0)),
        ),
        compiler_params=pltpu.CompilerParams(vmem_limit_bytes=40 << 20),
        cost_estimate=pl.CostEstimate(flops=TASKS * 24 * PATCH**3, bytes_accessed=TASKS * 8 * PATCH**2, transcendentals=0),
    )(pos, count, obj, probe, lefts, rights)


def inverse_kernel(last, pos_ref, order_ref, slot_ref, count_ref, far_ref, frame_ref, probe_ref, left_ref, right_ref, *rest):
    if last:
        perm_ref, before_ref, out_ref, acc_ref, even_ref, odd_ref = rest
    else:
        (acc_ref,) = rest
    i = pl.program_id(0)

    @pl.when(i == 0)
    def _():
        if last:
            acc_ref[...] = before_ref[...]
        else:
            acc_ref[...] = jnp.zeros_like(acc_ref)

    @pl.when(i < count_ref[0])
    def _():
        block, offset, rows = window(pos_ref, order_ref[i])
        weighted = []
        for h in range(2):
            re = far_ref[0, h, :HALF, :]
            im = far_ref[0, h, HALF:, :]
            weight = re * re + im * im - frame_ref[0, h * HALF : (h + 1) * HALF, :]
            weighted.append(jnp.concatenate([weight * re, weight * im], axis=0))
        back = [
            left_dot(right_ref[0], weighted[0] + weighted[1]),
            left_dot(right_ref[1], weighted[0] - weighted[1]),
        ]
        low = [jnp.concatenate([b[:HALF, :HALF], b[HALF:, :HALF]], axis=1) for b in back]
        high = [jnp.concatenate([b[:HALF, HALF:], b[HALF:, HALF:]], axis=1) for b in back]
        low = jnp.concatenate(low, axis=0)
        high = jnp.concatenate(high, axis=0)
        chis = [right_dot(low + high, left_ref[0]), right_dot(low - high, left_ref[1])]
        for p in range(2):
            mask = lane_mask(offset, p)
            for q in range(2):
                parity, first = rows[q]
                w = rolled_probe(probe_ref, offset, p, q)
                re = chis[p][q * HALF : (q + 1) * HALF, :HALF]
                im = chis[p][q * HALF : (q + 1) * HALF, HALF:]
                g = [w[0] * re + w[1] * im, w[0] * im - w[1] * re]
                for c in range(2):
                    here = (c, p, block, parity, pl.ds(first, HALF), slice(None))
                    acc_ref[here] = acc_ref[here] + jnp.where(mask, g[c], 0.0)
                    there = (c, p, block + 1, parity, pl.ds(first, HALF), slice(None))
                    acc_ref[there] = acc_ref[there] + jnp.where(mask, 0.0, g[c])

    if last:

        @pl.when(i == pl.num_programs(0) - 1)
        def _():
            for c in range(2):
                for b in range(BLOCKS):
                    for q in range(2):
                        even_ref[pl.ds(q, EXT // 2, stride=2), :] = acc_ref[c, 0, b, q]
                        odd_ref[pl.ds(q, EXT // 2, stride=2), :] = acc_ref[c, 1, b, q]
                    mixed = jnp.concatenate([even_ref[...], odd_ref[...]], axis=1)
                    out_ref[c, :, b * PATCH : (b + 1) * PATCH] = three_dot(mixed, perm_ref[...])


def inverse(last, most, pos, order, slot, count, far, frames, probe, lefts, rights, before=None):
    whole = pl.BlockSpec(memory_space=pltpu.VMEM)
    parts = (2, 2, BLOCKS, 2, EXT // 2, HALF)
    more = (jnp.asarray(shuffle().T.copy()), before) if last else ()
    strips = [pltpu.VMEM(parts, f32)] + [pltpu.VMEM((EXT, HALF), f32)] * 2
    return pl.pallas_call(
        functools.partial(inverse_kernel, last),
        out_shape=jax.ShapeDtypeStruct((2, EXT, EXT) if last else parts, f32),
        grid_spec=pltpu.PrefetchScalarGridSpec(
            num_scalar_prefetch=4,
            grid=(most,),
            in_specs=[
                pl.BlockSpec((1, 2, PATCH, PATCH), lambda i, pos, order, slot, count: (order[i], 0, 0, 0)),
                pl.BlockSpec((1, PATCH, PATCH), lambda i, pos, order, slot, count: (slot[i], 0, 0)),
            ]
            + [whole] * (3 + len(more)),
            out_specs=whole,
            scratch_shapes=strips if last else [],
        ),
        compiler_params=pltpu.CompilerParams(vmem_limit_bytes=40 << 20),
        cost_estimate=pl.CostEstimate(flops=most * 24 * PATCH**3, bytes_accessed=most * 12 * PATCH**2, transcendentals=0),
    )(pos, order, slot, count, far, frames, probe, lefts, rights, *more)


def extended_2(block, sides, width):
    for axis, dim in sides:
        count = lax.axis_size(axis)
        forward_pairs = [(i, i + 1) for i in range(count - 1)]
        backward_pairs = [(target, source) for source, target in forward_pairs]
        low = lax.ppermute(lax.slice_in_dim(block, block.shape[dim] - width, None, axis=dim), axis, forward_pairs)
        high = lax.ppermute(lax.slice_in_dim(block, 0, width, axis=dim), axis, backward_pairs)
        block = jnp.concatenate([low, block, high], axis=dim)
    return block


def exchanged(first, last, axis):
    count = lax.axis_size(axis)
    up = [(i, i + 1) for i in range(count - 1)]
    down = [(i + 1, i) for i in range(count - 1)]
    return lax.ppermute(last, axis, up), lax.ppermute(first, axis, down)


def ordered(chosen, helper_cols, most):
    task_ids = jnp.arange(TASKS, dtype=jnp.int32)
    place = jnp.sum(jnp.logical_and(chosen[None, :], task_ids[None, :] < task_ids[:, None]), axis=1)
    spot = jnp.logical_and(chosen[None, :], place[None, :] == jnp.arange(most)[:, None])
    order = jnp.sum(jnp.where(spot, task_ids[None, :], 0), axis=1).astype(jnp.int32)
    slot = jnp.sum(jnp.where(spot, helper_cols[None, :], 0), axis=1).astype(jnp.int32)
    return order, slot, jnp.sum(chosen).astype(jnp.int32).reshape(1)


def local(extended, probe, arrived_0, arrived_1, offsets, helper_cols, count):
    task_ids = jnp.arange(TASKS, dtype=jnp.int32)
    same = helper_cols[:, None] == helper_cols[None, :]
    second = jnp.any(jnp.logical_and(same, task_ids[None, :] < task_ids[:, None]), axis=1)
    valid = task_ids < count[0]
    order_0 = ordered(jnp.logical_and(valid, jnp.logical_not(second)), helper_cols, 16)
    order_1 = ordered(jnp.logical_and(valid, second), helper_cols, TASKS // 2)
    lefts, rights = tables()
    obj = prep(extended)
    pro = prep(probe)
    far = forward(offsets, count, obj, pro, lefts, rights)
    part = inverse(False, 16, offsets, *order_0, far, arrived_0, pro, lefts, rights)
    return inverse(True, TASKS // 2, offsets, *order_1, far, arrived_1, pro, lefts, rights, part)


def per_device(object_field, probe, frames, positions, helpers, task_counts):
    extended = extended_2(object_field, (("gx", 2),), HALF)
    kept = frames[0, 0]
    arrived = lax.all_to_all(kept[:, 0], "gx", split_axis=0, concat_axis=0, tiled=True)
    arrived_1 = lax.all_to_all(kept[:, 1], "gx", split_axis=0, concat_axis=0, tiled=True)
    extended = extended_2(extended, (("gy", 1),), HALF)
    total = local(
        extended,
        probe,
        arrived,
        arrived_1,
        positions[0, 0].reshape(-1),
        helpers[0, 0, :, 0],
        task_counts[0],
    )

    tile = object_field.shape[1]
    left_in, right_in = exchanged(total[:, :, :HALF], total[:, :, HALF + tile :], "gx")
    middle = total[:, :, HALF : HALF + tile]
    middle = middle.at[:, :, :HALF].add(left_in)
    middle = middle.at[:, :, tile - HALF :].add(right_in)
    up_in, down_in = exchanged(middle[:, :HALF, :], middle[:, HALF + tile :, :], "gy")
    gradient = middle[:, HALF : HALF + tile, :]
    gradient = gradient.at[:, :HALF, :].add(up_in)
    gradient = gradient.at[:, tile - HALF :, :].add(down_in)
    return object_field - step_size * (gradient + ridge * object_field)


def solution(mesh):
    in_specs = (
        P(None, "gy", "gx"),
        P(),
        P("gy", "gx", None, None, None, None),
        P("gy", "gx", None, None),
        P("gy", "gx", None, None),
        P("gy", "gx"),
    )
    out_specs = P(None, "gy", "gx")
    return jax.shard_map(per_device, mesh=mesh, in_specs=in_specs, out_specs=out_specs, check_vma=False)
```

```python
import functools

import jax
import jax.numpy as jnp
import ml_dtypes
import numpy as np
from jax import lax
from jax.experimental import pallas as pl
from jax.experimental.pallas import tpu as pltpu
from jax.sharding import PartitionSpec as P


PATCH = 256
HALF = 128
TASKS = 24
TILE = 512
BLOCKS = 3
EXT = 768


step_size = 0.1
ridge = 0.5

f32 = jnp.float32
bf16 = jnp.bfloat16


def tables():
    j = np.arange(HALF)
    even = np.exp(-2j * np.pi * (np.outer(j, 2 * j) % PATCH) / PATCH) / 16.0
    odd = np.exp(-2j * np.pi * (np.outer(j, 2 * j + 1) % PATCH) / PATCH) / 16.0

    def left(w):
        return np.block([[w.real, -w.imag], [w.imag, w.real]])

    def split(w):
        high = w.astype(ml_dtypes.bfloat16)
        low = (w - high.astype(np.float64)).astype(ml_dtypes.bfloat16)
        return high, low

    pairs = [split(left(w)) for w in (even, odd)]
    lefts = np.stack([np.stack(pair) for pair in pairs])
    return jnp.asarray(lefts), jnp.asarray(np.swapaxes(lefts, 2, 3).copy())


def shuffle():
    p = np.zeros((PATCH, PATCH), np.float32)
    j = np.arange(HALF)
    p[2 * j, j] = 1
    p[2 * j + 1, HALF + j] = 1
    return p.astype(ml_dtypes.bfloat16)


def two_terms(x):
    high = x.astype(bf16)
    low = (x - high.astype(f32)).astype(bf16)
    return high, low


def three_dot(x, p):
    high = x.astype(bf16)
    rest = x - high.astype(f32)
    mid = rest.astype(bf16)
    low = (rest - mid.astype(f32)).astype(bf16)
    out = jnp.dot(high, p, preferred_element_type=f32)
    out = out + jnp.dot(mid, p, preferred_element_type=f32)
    return out + jnp.dot(low, p, preferred_element_type=f32)


def spread(value, perm_ref, out_ref, c, b, even_ref, odd_ref):
    rows = value.shape[0]
    mixed = three_dot(value, perm_ref[...])
    even_ref[:rows] = mixed[:, :HALF]
    odd_ref[:rows] = mixed[:, HALF:]
    for q in range(2):
        out_ref[c, 0, b, q] = even_ref[pl.ds(q, rows // 2, stride=2), :]
        out_ref[c, 1, b, q] = odd_ref[pl.ds(q, rows // 2, stride=2), :]


def prep_kernel(*refs):
    perm_ref, probe_out, out_ref, even_ref, odd_ref = refs[6:11]
    probe_ref, tile_ref, left_ref, right_ref, up_ref, down_ref = refs[11:17]
    copies = [pltpu.make_async_copy(refs[i], refs[11 + i], refs[17].at[i]) for i in range(6)]
    for copy in copies:
        copy.start()
    for copy in copies:
        copy.wait()
    size = tile_ref.shape[2]
    for c in range(2):
        spread(probe_ref[c], perm_ref, probe_out, c, 0, even_ref, odd_ref)
        for b in range(BLOCKS):
            if b == 0:
                middle = jnp.concatenate([left_ref[c], tile_ref[c, :, :HALF]], axis=1)
            elif b == 1:
                middle = tile_ref[c, :, HALF : size - HALF]
            else:
                middle = jnp.concatenate([tile_ref[c, :, size - HALF :], right_ref[c]], axis=1)
            cols = slice(b * PATCH, (b + 1) * PATCH)
            value = jnp.concatenate([up_ref[c, :, cols], middle, down_ref[c, :, cols]], axis=0)
            spread(value, perm_ref, out_ref, c, b, even_ref, odd_ref)


def prep(probe, pieces):
    return pl.pallas_call(
        prep_kernel,
        out_shape=(
            jax.ShapeDtypeStruct((2, 2, 1, 2, HALF, HALF), f32),
            jax.ShapeDtypeStruct((2, 2, BLOCKS, 2, EXT // 2, HALF), f32),
        ),
        in_specs=[pl.BlockSpec(memory_space=pl.ANY)] * 6 + [pl.BlockSpec(memory_space=pltpu.VMEM)],
        out_specs=[pl.BlockSpec(memory_space=pltpu.VMEM)] * 2,
        scratch_shapes=[pltpu.VMEM((EXT, HALF), f32)] * 2
        + [pltpu.VMEM(x.shape, f32) for x in (probe, *pieces)]
        + [pltpu.SemaphoreType.DMA((6,))],
        compiler_params=pltpu.CompilerParams(vmem_limit_bytes=40 << 20),
        cost_estimate=pl.CostEstimate(flops=6 * EXT * EXT * PATCH * 2, bytes_accessed=16 * EXT * EXT, transcendentals=0),
    )(probe, *pieces, jnp.asarray(shuffle()))


def window(pos_ref, t):
    start_y = pos_ref[2 * t] + HALF
    start_x = pos_ref[2 * t + 1] + HALF
    block = jnp.where(start_x >= PATCH, 1, 0)
    offset = start_x - block * PATCH
    rows = [((start_y + q) & 1, (start_y + q) >> 1) for q in range(2)]
    return block, offset, rows


def rolled_probe(probe_ref, offset, p, q):
    source = (p + offset) & 1
    amount = ((offset + source - p) >> 1) & (HALF - 1)
    return [pltpu.roll(probe_ref[c, source, 0, q], amount, 1) for c in range(2)]


def lane_mask(offset, p):
    lane = lax.broadcasted_iota(jnp.int32, (HALF, HALF), 1)
    return lane >= ((offset + 1 - p) >> 1)


def put(high_ref, low_ref, where, value):
    high, low = two_terms(value)
    high_ref[where] = high
    low_ref[where] = low


def right_from(high_ref, low_ref, k, w_ref):
    high = high_ref[k]
    w = w_ref[k, 0]
    out = jnp.dot(
        jnp.concatenate([high, low_ref[k], high], axis=1),
        jnp.concatenate([w, w, w_ref[k, 1]], axis=0),
        preferred_element_type=f32,
    )
    return out


def left_from(w_ref, high_ref, low_ref, k):
    high = high_ref[k]
    w = w_ref[k, 0]
    return jnp.dot(
        jnp.concatenate([w, w, w_ref[k, 1]], axis=1),
        jnp.concatenate([high, low_ref[k], high], axis=0),
        preferred_element_type=f32,
    )


def forward_kernel(pos_ref, count_ref, obj_ref, probe_ref, left_ref, right_ref, out_ref, *scratch):
    step = pl.program_id(0)

    @pl.when(2 * step < count_ref[0])
    def _():
        for k in range(2):
            ah_ref, al_ref = scratch[4 * k : 4 * k + 2]
            block, offset, rows = window(pos_ref, 2 * step + k)
            for p in range(2):
                mask = lane_mask(offset, p)
                for q in range(2):
                    parity, first = rows[q]
                    o = [
                        jnp.where(
                            mask,
                            obj_ref[c, p, block, parity, pl.ds(first, HALF), :],
                            obj_ref[c, p, block + 1, parity, pl.ds(first, HALF), :],
                        )
                        for c in range(2)
                    ]
                    w = rolled_probe(probe_ref, offset, p, q)
                    r = slice(q * HALF, (q + 1) * HALF)
                    put(ah_ref, al_ref, (p, r, slice(0, HALF)), w[0] * o[0] - w[1] * o[1])
                    put(ah_ref, al_ref, (p, r, slice(HALF, PATCH)), w[0] * o[1] + w[1] * o[0])
        for k in range(2):
            ah_ref, al_ref, bh_ref, bl_ref = scratch[4 * k : 4 * k + 4]
            even = right_from(ah_ref, al_ref, 0, right_ref)
            odd = right_from(ah_ref, al_ref, 1, right_ref)
            for q in range(2):
                r = slice(q * HALF, (q + 1) * HALF)
                for c in range(2):
                    lanes = slice(c * HALF, (c + 1) * HALF)
                    put(bh_ref, bl_ref, (q, lanes, slice(0, HALF)), even[r, lanes] + odd[r, lanes])
                    put(bh_ref, bl_ref, (q, lanes, slice(HALF, PATCH)), even[r, lanes] - odd[r, lanes])
        for k in range(2):
            bh_ref, bl_ref = scratch[4 * k + 2 : 4 * k + 4]
            even = left_from(left_ref, bh_ref, bl_ref, 0)
            odd = left_from(left_ref, bh_ref, bl_ref, 1)
            out_ref[k, 0] = even + odd
            out_ref[k, 1] = even - odd


def forward(pos, count, obj, probe, lefts, rights):
    whole = pl.BlockSpec(memory_space=pltpu.VMEM)
    return pl.pallas_call(
        forward_kernel,
        out_shape=jax.ShapeDtypeStruct((TASKS, 2, PATCH, PATCH), f32),
        grid_spec=pltpu.PrefetchScalarGridSpec(
            num_scalar_prefetch=2,
            grid=(TASKS // 2,),
            in_specs=[whole] * 4,
            out_specs=pl.BlockSpec((2, 2, PATCH, PATCH), lambda t, pos, count: (t, 0, 0, 0)),
            scratch_shapes=[pltpu.VMEM((2, PATCH, PATCH), bf16)] * 8,
        ),
        compiler_params=pltpu.CompilerParams(vmem_limit_bytes=40 << 20),
        cost_estimate=pl.CostEstimate(flops=TASKS * 24 * PATCH**3, bytes_accessed=TASKS * 8 * PATCH**2, transcendentals=0),
    )(pos, count, obj, probe, lefts, rights)


def inverse_kernel(last, pos_ref, order_ref, slot_ref, count_ref, far_0, far_1, frame_0, frame_1, probe_ref, left_ref, right_ref, *rest):
    if last:
        perm_ref, before_ref = rest[:2]
        outs = rest[2:7]
        scratch = rest[7:15]
        acc_ref, even_ref, odd_ref, earlier_ref, sem = rest[15:]
        load = pltpu.make_async_copy(before_ref, earlier_ref, sem)
    else:
        acc_ref = rest[0]
        scratch = rest[1:]
    i = pl.program_id(0)

    @pl.when(i == 0)
    def _():
        if last:
            load.start()
        acc_ref[...] = jnp.zeros_like(acc_ref)

    @pl.when(2 * i < count_ref[0])
    def _():
        for k, far_ref, frame_ref in ((0, far_0, frame_0), (1, far_1, frame_1)):
            sh_ref, sl_ref = scratch[4 * k : 4 * k + 2]
            step = 32
            for at in range(0, HALF, step):
                parts = []
                for h in range(2):
                    re = far_ref[0, h, at : at + step, :]
                    im = far_ref[0, h, HALF + at : HALF + at + step, :]
                    weight = re * re + im * im - frame_ref[0, h * HALF + at : h * HALF + at + step, :]
                    parts.append((weight * re, weight * im))
                for c in range(2):
                    r = slice(c * HALF + at, c * HALF + at + step)
                    put(sh_ref, sl_ref, (0, r), parts[0][c] + parts[1][c])
                    put(sh_ref, sl_ref, (1, r), parts[0][c] - parts[1][c])
        for k in range(2):
            sh_ref, sl_ref, th_ref, tl_ref = scratch[4 * k : 4 * k + 4]
            for q in range(2):
                back = left_from(right_ref, sh_ref, sl_ref, q)
                r = slice(q * HALF, (q + 1) * HALF)
                for c in range(2):
                    lanes = slice(c * HALF, (c + 1) * HALF)
                    low, high = back[lanes, :HALF], back[lanes, HALF:]
                    put(th_ref, tl_ref, (0, r, lanes), low + high)
                    put(th_ref, tl_ref, (1, r, lanes), low - high)
        for k in range(2):
            th_ref, tl_ref = scratch[4 * k + 2 : 4 * k + 4]
            block, offset, rows = window(pos_ref, order_ref[2 * i + k])
            live = 2 * i + k < count_ref[0]
            for p in range(2):
                chi = right_from(th_ref, tl_ref, p, left_ref)
                mask = lane_mask(offset, p)
                for q in range(2):
                    parity, first = rows[q]
                    w = rolled_probe(probe_ref, offset, p, q)
                    r = slice(q * HALF, (q + 1) * HALF)
                    re, im = chi[r, :HALF], chi[r, HALF:]
                    g = [w[0] * re + w[1] * im, w[0] * im - w[1] * re]
                    for c in range(2):
                        here = acc_ref.at[c, p, block, parity, pl.ds(first, HALF), :]
                        there = acc_ref.at[c, p, block + 1, parity, pl.ds(first, HALF), :]
                        value = jnp.where(mask, here[...], there[...]) + g[c]
                        pltpu.store(here, value, mask=jnp.logical_and(mask, live))
                        pltpu.store(there, value, mask=jnp.logical_and(jnp.logical_not(mask), live))

    if last:

        @pl.when(i == pl.num_programs(0) - 1)
        def _():
            load.wait()
            for c in range(2):
                for b in range(BLOCKS):
                    for q in range(2):
                        even_ref[pl.ds(q, EXT // 2, stride=2), :] = acc_ref[c, 0, b, q] + earlier_ref[c, 0, b, q]
                        odd_ref[pl.ds(q, EXT // 2, stride=2), :] = acc_ref[c, 1, b, q] + earlier_ref[c, 1, b, q]
                    high, low = two_terms(jnp.concatenate([even_ref[...], odd_ref[...]], axis=1))
                    value = jnp.dot(high, perm_ref[...], preferred_element_type=f32)
                    value = value + jnp.dot(low, perm_ref[...], preferred_element_type=f32)
                    cols = slice(b * PATCH, (b + 1) * PATCH)
                    outs[3][c, :, cols] = value[:HALF]
                    outs[4][c, :, cols] = value[HALF + TILE :]
                    middle = value[HALF : HALF + TILE]
                    if b == 0:
                        outs[1][c] = middle[:, :HALF]
                        outs[0][c, :, :HALF] = middle[:, HALF:]
                    elif b == 1:
                        outs[0][c, :, HALF : HALF + PATCH] = middle
                    else:
                        outs[0][c, :, HALF + PATCH :] = middle[:, :HALF]
                        outs[2][c] = middle[:, HALF:]


def inverse(last, most, pos, order, slot, count, far, frames, probe, lefts, rights, before=None):
    whole = pl.BlockSpec(memory_space=pltpu.VMEM)
    parts = (2, 2, BLOCKS, 2, EXT // 2, HALF)
    more = (jnp.asarray(shuffle().T.copy()), before) if last else ()
    more_specs = [whole, pl.BlockSpec(memory_space=pl.ANY)] if last else []
    strips = [pltpu.VMEM(parts, f32)] + [pltpu.VMEM((EXT, HALF), f32)] * 2 + [pltpu.VMEM(parts, f32), pltpu.SemaphoreType.DMA]

    sizes = ((TILE, TILE), (TILE, HALF), (TILE, HALF), (HALF, EXT), (HALF, EXT))

    def far_spec(k):
        return pl.BlockSpec((1, 2, PATCH, PATCH), lambda i, pos, order, slot, count: (order[2 * i + k], 0, 0, 0))

    def frame_spec(k):
        return pl.BlockSpec((1, PATCH, PATCH), lambda i, pos, order, slot, count: (slot[2 * i + k], 0, 0))

    return pl.pallas_call(
        functools.partial(inverse_kernel, last),
        out_shape=[jax.ShapeDtypeStruct((2,) + size, f32) for size in sizes] if last else jax.ShapeDtypeStruct(parts, f32),
        grid_spec=pltpu.PrefetchScalarGridSpec(
            num_scalar_prefetch=4,
            grid=(most // 2,),
            in_specs=[far_spec(0), far_spec(1), frame_spec(0), frame_spec(1)] + [whole] * 3 + more_specs,
            out_specs=[whole] * 5 if last else whole,
            scratch_shapes=[pltpu.VMEM((2, PATCH, PATCH), bf16)] * 8 + (strips if last else []),
        ),
        compiler_params=pltpu.CompilerParams(vmem_limit_bytes=40 << 20),
        cost_estimate=pl.CostEstimate(flops=most * 24 * PATCH**3, bytes_accessed=most * 12 * PATCH**2, transcendentals=0),
    )(pos, order, slot, count, far, far, frames, frames, probe, lefts, rights, *more)


def strips_kernel(object_ref, first_ref, last_ref, sem):
    size = object_ref.shape[2]
    copies = [
        pltpu.make_async_copy(object_ref.at[:, :, pl.ds(0, HALF)], first_ref, sem.at[0]),
        pltpu.make_async_copy(object_ref.at[:, :, pl.ds(size - HALF, HALF)], last_ref, sem.at[1]),
    ]
    for copy in copies:
        copy.start()
    for copy in copies:
        copy.wait()


def strips(block):
    strip = jax.ShapeDtypeStruct((2, block.shape[1], HALF), f32)
    return pl.pallas_call(
        strips_kernel,
        out_shape=(strip, strip),
        in_specs=[pl.BlockSpec(memory_space=pl.ANY)],
        out_specs=[pl.BlockSpec(memory_space=pltpu.VMEM)] * 2,
        scratch_shapes=[pltpu.SemaphoreType.DMA((2,))],
        compiler_params=pltpu.CompilerParams(vmem_limit_bytes=62 << 20),
        cost_estimate=pl.CostEstimate(flops=0, bytes_accessed=2 << 20, transcendentals=0),
    )(block)


def pick_kernel(slot, frames_ref, out_ref, buffer_ref, sem):
    count = sem.shape[1]
    size = out_ref.shape[0] // count
    pieces = [pl.ds(i * size, size) for i in range(count)]
    loads = [pltpu.make_async_copy(frames_ref.at[p, slot], buffer_ref.at[p], sem.at[0, i]) for i, p in enumerate(pieces)]
    stores = [pltpu.make_async_copy(buffer_ref.at[p], out_ref.at[p], sem.at[1, i]) for i, p in enumerate(pieces)]
    for load in loads:
        load.start()
    for load, store in zip(loads, stores):
        load.wait()
        store.start()
    for store in stores:
        store.wait()


def pick(kept, slot):
    shape = (kept.shape[0], PATCH, PATCH)
    return pl.pallas_call(
        functools.partial(pick_kernel, slot),
        out_shape=jax.ShapeDtypeStruct(shape, f32),
        in_specs=[pl.BlockSpec(memory_space=pl.ANY)],
        out_specs=pl.BlockSpec(memory_space=pl.ANY),
        scratch_shapes=[pltpu.VMEM(shape, f32), pltpu.SemaphoreType.DMA((2, 4))],
        compiler_params=pltpu.CompilerParams(vmem_limit_bytes=58 << 20),
        cost_estimate=pl.CostEstimate(flops=0, bytes_accessed=8 << 20, transcendentals=0),
    )(kept)


def from_tile(sent, dy, dx):
    high, wide = lax.axis_size("gy"), lax.axis_size("gx")
    if dy == 0:
        return lax.ppermute(sent, "gx", [(i + dx, i) for i in range(wide) if 0 <= i + dx < wide])
    return lax.ppermute(sent, "gy", [(i + dy, i) for i in range(high) if 0 <= i + dy < high])


def final_kernel(object_ref, total_ref, left_ref, right_ref, up_ref, down_ref, left_ends, right_ends, out_ref):
    out_ref[...] = (1.0 - step_size * ridge) * object_ref[...] - step_size * total_ref[...]
    top, bottom = slice(0, HALF), slice(TILE - HALF, TILE)
    for rows, ref, at in ((top, up_ref, 0), (bottom, down_ref, HALF)):
        out_ref[:, rows, :] = out_ref[:, rows, :] - step_size * ref[:, :, HALF : HALF + TILE]
        for lanes, ends in ((top, left_ends), (bottom, right_ends)):
            out_ref[:, rows, lanes] = out_ref[:, rows, lanes] - step_size * ends[:, at : at + HALF]
    out_ref[:, :, top] = out_ref[:, :, top] - step_size * left_ref[...]
    out_ref[:, :, bottom] = out_ref[:, :, bottom] - step_size * right_ref[...]


def final(block, *parts):
    return pl.pallas_call(
        final_kernel,
        out_shape=jax.ShapeDtypeStruct(block.shape, f32),
        in_specs=[pl.BlockSpec(memory_space=pltpu.VMEM)] * 8,
        out_specs=pl.BlockSpec(memory_space=pltpu.VMEM),
        compiler_params=pltpu.CompilerParams(vmem_limit_bytes=16 << 20),
        cost_estimate=pl.CostEstimate(flops=4 * block.size, bytes_accessed=16 * block.size, transcendentals=0),
    )(block, *parts)


def ordered(chosen, helper_cols, most):
    task_ids = jnp.arange(TASKS, dtype=jnp.int32)
    place = jnp.sum(jnp.logical_and(chosen[None, :], task_ids[None, :] < task_ids[:, None]), axis=1)
    spot = jnp.logical_and(chosen[None, :], place[None, :] == jnp.arange(most)[:, None])
    order = jnp.sum(jnp.where(spot, task_ids[None, :], 0), axis=1).astype(jnp.int32)
    slot = jnp.sum(jnp.where(spot, helper_cols[None, :], 0), axis=1).astype(jnp.int32)
    return order, slot, jnp.sum(chosen).astype(jnp.int32).reshape(1)


def local(pieces, probe, arrived_0, arrived_1, offsets, helper_cols, count):
    task_ids = jnp.arange(TASKS, dtype=jnp.int32)
    same = helper_cols[:, None] == helper_cols[None, :]
    second = jnp.any(jnp.logical_and(same, task_ids[None, :] < task_ids[:, None]), axis=1)
    valid = task_ids < count[0]
    order_0 = ordered(jnp.logical_and(valid, jnp.logical_not(second)), helper_cols, 16)
    order_1 = ordered(jnp.logical_and(valid, second), helper_cols, TASKS // 2)
    lefts, rights = tables()
    pro, obj = prep(probe, pieces)
    far = forward(offsets, count, obj, pro, lefts, rights)
    part = inverse(False, 16, offsets, *order_0, far, arrived_0, pro, lefts, rights)
    return inverse(True, TASKS // 2, offsets, *order_1, far, arrived_1, pro, lefts, rights, part)


def per_device(object_field, probe, frames, positions, helpers, task_counts):
    first, last = strips(object_field)
    kept = frames[0, 0]
    left, right = from_tile(last, 0, -1), from_tile(first, 0, 1)
    arrived_0 = lax.all_to_all(pick(kept, 0), "gx", split_axis=0, concat_axis=0, tiled=True)
    again, _ = lax.optimization_barrier((kept, arrived_0))
    arrived_1 = lax.all_to_all(pick(again, 1), "gx", split_axis=0, concat_axis=0, tiled=True)
    above = jnp.concatenate([left[:, -HALF:], object_field[:, -HALF:], right[:, -HALF:]], axis=2)
    below = jnp.concatenate([left[:, :HALF], object_field[:, :HALF], right[:, :HALF]], axis=2)
    up, down = from_tile(above, -1, 0), from_tile(below, 1, 0)
    parts = local(
        [object_field, left, right, up, down],
        probe,
        arrived_0,
        arrived_1,
        positions[0, 0].reshape(-1),
        helpers[0, 0, :, 0],
        task_counts[0],
    )
    middle, to_left, to_right, to_up, to_down = parts
    up, down = from_tile(to_down, -1, 0), from_tile(to_up, 1, 0)
    left, right = from_tile(to_right, 0, -1), from_tile(to_left, 0, 1)
    first_ends = jnp.concatenate([up[:, :, :HALF], down[:, :, :HALF]], axis=1)
    last_ends = jnp.concatenate([up[:, :, -HALF:], down[:, :, -HALF:]], axis=1)
    left_ends, right_ends = from_tile(last_ends, 0, -1), from_tile(first_ends, 0, 1)
    return final(object_field, middle, left, right, up, down, left_ends, right_ends)


def solution(mesh):
    in_specs = (
        P(None, "gy", "gx"),
        P(),
        P("gy", "gx", None, None, None, None),
        P("gy", "gx", None, None),
        P("gy", "gx", None, None),
        P("gy", "gx"),
    )
    out_specs = P(None, "gy", "gx")
    return jax.shard_map(per_device, mesh=mesh, in_specs=in_specs, out_specs=out_specs, check_vma=False)
```

```python
import functools

import jax
import jax.numpy as jnp
import ml_dtypes
import numpy as np
from jax import lax
from jax.experimental import pallas as pl
from jax.experimental.pallas import tpu as pltpu
from jax.sharding import PartitionSpec as P


PATCH = 256
HALF = 128
TASKS = 24
TILE = 512
BLOCKS = 3
EXT = 768


step_size = 0.1
ridge = 0.5

f32 = jnp.float32
bf16 = jnp.bfloat16


def tables():
    j = np.arange(HALF)
    even = np.exp(-2j * np.pi * (np.outer(j, 2 * j) % PATCH) / PATCH) / 16.0
    odd = np.exp(-2j * np.pi * (np.outer(j, 2 * j + 1) % PATCH) / PATCH) / 16.0

    def left(w):
        return np.block([[w.real, -w.imag], [w.imag, w.real]])

    def split(w):
        high = w.astype(ml_dtypes.bfloat16)
        low = (w - high.astype(np.float64)).astype(ml_dtypes.bfloat16)
        return high, low

    pairs = [split(left(w)) for w in (even, odd)]
    lefts = np.stack([np.stack(pair) for pair in pairs])
    return jnp.asarray(lefts), jnp.asarray(np.swapaxes(lefts, 2, 3).copy())


def shuffle():
    p = np.zeros((PATCH, PATCH), np.float32)
    j = np.arange(HALF)
    p[2 * j, j] = 1
    p[2 * j + 1, HALF + j] = 1
    return p.astype(ml_dtypes.bfloat16)


def two_terms(x):
    high = x.astype(bf16)
    low = (x - high.astype(f32)).astype(bf16)
    return high, low


def three_dot(x, p):
    high = x.astype(bf16)
    rest = x - high.astype(f32)
    mid = rest.astype(bf16)
    low = (rest - mid.astype(f32)).astype(bf16)
    out = jnp.dot(high, p, preferred_element_type=f32)
    out = out + jnp.dot(mid, p, preferred_element_type=f32)
    return out + jnp.dot(low, p, preferred_element_type=f32)


def spread(value, perm_ref, out_ref, c, b, even_ref, odd_ref):
    rows = value.shape[0]
    mixed = three_dot(value, perm_ref[...])
    even_ref[:rows] = mixed[:, :HALF]
    odd_ref[:rows] = mixed[:, HALF:]
    for q in range(2):
        out_ref[c, 0, b, q] = even_ref[pl.ds(q, rows // 2, stride=2), :]
        out_ref[c, 1, b, q] = odd_ref[pl.ds(q, rows // 2, stride=2), :]


def middle_kernel(probe_ref, tile_ref, left_ref, right_ref, perm_ref, probe_out, out_ref, even_ref, odd_ref):
    size = tile_ref.shape[2]
    for c in range(2):
        spread(probe_ref[c], perm_ref, probe_out, c, 0, even_ref, odd_ref)
        for b in range(BLOCKS):
            if b == 0:
                value = jnp.concatenate([left_ref[c], tile_ref[c, :, :HALF]], axis=1)
            elif b == 1:
                value = tile_ref[c, :, HALF : size - HALF]
            else:
                value = jnp.concatenate([tile_ref[c, :, size - HALF :], right_ref[c]], axis=1)
            spread(value, perm_ref, out_ref, c, b, even_ref, odd_ref)


def middle_rows(probe, tile, left, right):
    whole = pl.BlockSpec(memory_space=pltpu.VMEM)
    return pl.pallas_call(
        middle_kernel,
        out_shape=(
            jax.ShapeDtypeStruct((2, 2, 1, 2, HALF, HALF), f32),
            jax.ShapeDtypeStruct((2, 2, BLOCKS, 2, TILE // 2, HALF), f32),
        ),
        in_specs=[whole] * 5,
        out_specs=[whole] * 2,
        scratch_shapes=[pltpu.VMEM((TILE, HALF), f32)] * 2,
        compiler_params=pltpu.CompilerParams(vmem_limit_bytes=30 << 20),
        cost_estimate=pl.CostEstimate(flops=6 * TILE * EXT * PATCH * 2, bytes_accessed=16 * TILE * EXT, transcendentals=0),
    )(probe, tile, left, right, jnp.asarray(shuffle()))


def ends_kernel(up_ref, down_ref, perm_ref, out_ref, even_ref, odd_ref):
    for side, ref in enumerate((up_ref, down_ref)):
        for c in range(2):
            for b in range(BLOCKS):
                spread(ref[c, :, b * PATCH : (b + 1) * PATCH], perm_ref, out_ref.at[side], c, b, even_ref, odd_ref)


def end_rows(up, down):
    whole = pl.BlockSpec(memory_space=pltpu.VMEM)
    return pl.pallas_call(
        ends_kernel,
        out_shape=jax.ShapeDtypeStruct((2, 2, 2, BLOCKS, 2, HALF // 2, HALF), f32),
        in_specs=[whole] * 3,
        out_specs=whole,
        scratch_shapes=[pltpu.VMEM((HALF, HALF), f32)] * 2,
        compiler_params=pltpu.CompilerParams(vmem_limit_bytes=30 << 20),
        cost_estimate=pl.CostEstimate(flops=6 * PATCH * EXT * PATCH * 2, bytes_accessed=16 * PATCH * EXT, transcendentals=0),
    )(up, down, jnp.asarray(shuffle()))


def window(pos_ref, t):
    start_y = pos_ref[2 * t] + HALF
    start_x = pos_ref[2 * t + 1] + HALF
    block = jnp.where(start_x >= PATCH, 1, 0)
    offset = start_x - block * PATCH
    rows = [((start_y + q) & 1, (start_y + q) >> 1) for q in range(2)]
    return block, offset, rows


def rolled_probe(probe_ref, offset, p, q):
    source = (p + offset) & 1
    amount = ((offset + source - p) >> 1) & (HALF - 1)
    return [pltpu.roll(probe_ref[c, source, 0, q], amount, 1) for c in range(2)]


def lane_mask(offset, p):
    lane = lax.broadcasted_iota(jnp.int32, (HALF, HALF), 1)
    return lane >= ((offset + 1 - p) >> 1)


def put(high_ref, low_ref, where, value):
    high, low = two_terms(value)
    high_ref[where] = high
    low_ref[where] = low


def right_from(high_ref, low_ref, k, w_ref):
    high = high_ref[k]
    w = w_ref[k, 0]
    out = jnp.dot(
        jnp.concatenate([high, low_ref[k], high], axis=1),
        jnp.concatenate([w, w, w_ref[k, 1]], axis=0),
        preferred_element_type=f32,
    )
    return out


def left_from(w_ref, high_ref, low_ref, k):
    high = high_ref[k]
    w = w_ref[k, 0]
    return jnp.dot(
        jnp.concatenate([w, w, w_ref[k, 1]], axis=1),
        jnp.concatenate([high, low_ref[k], high], axis=0),
        preferred_element_type=f32,
    )


def forward_kernel(pos_ref, count_ref, middle_ref, ends_ref, probe_ref, left_ref, right_ref, out_ref, obj_ref, sem, *scratch):
    step = pl.program_id(0)

    @pl.when(step == 0)
    def _():
        end = HALF // 2
        spans = ((ends_ref.at[0], 0, end), (middle_ref, end, TILE // 2), (ends_ref.at[1], end + TILE // 2, end))
        copies = [
            pltpu.make_async_copy(source, obj_ref.at[:, :, :, :, pl.ds(first, size), :], sem.at[k])
            for k, (source, first, size) in enumerate(spans)
        ]
        for copy in copies:
            copy.start()
        for copy in copies:
            copy.wait()

    @pl.when(2 * step < count_ref[0])
    def _():
        for k in range(2):
            ah_ref, al_ref = scratch[4 * k : 4 * k + 2]
            block, offset, rows = window(pos_ref, 2 * step + k)
            for p in range(2):
                mask = lane_mask(offset, p)
                for q in range(2):
                    parity, first = rows[q]
                    o = [
                        jnp.where(
                            mask,
                            obj_ref[c, p, block, parity, pl.ds(first, HALF), :],
                            obj_ref[c, p, block + 1, parity, pl.ds(first, HALF), :],
                        )
                        for c in range(2)
                    ]
                    w = rolled_probe(probe_ref, offset, p, q)
                    r = slice(q * HALF, (q + 1) * HALF)
                    put(ah_ref, al_ref, (p, r, slice(0, HALF)), w[0] * o[0] - w[1] * o[1])
                    put(ah_ref, al_ref, (p, r, slice(HALF, PATCH)), w[0] * o[1] + w[1] * o[0])
        for k in range(2):
            ah_ref, al_ref, bh_ref, bl_ref = scratch[4 * k : 4 * k + 4]
            even = right_from(ah_ref, al_ref, 0, right_ref)
            odd = right_from(ah_ref, al_ref, 1, right_ref)
            for q in range(2):
                r = slice(q * HALF, (q + 1) * HALF)
                for c in range(2):
                    lanes = slice(c * HALF, (c + 1) * HALF)
                    put(bh_ref, bl_ref, (q, lanes, slice(0, HALF)), even[r, lanes] + odd[r, lanes])
                    put(bh_ref, bl_ref, (q, lanes, slice(HALF, PATCH)), even[r, lanes] - odd[r, lanes])
        for k in range(2):
            bh_ref, bl_ref = scratch[4 * k + 2 : 4 * k + 4]
            even = left_from(left_ref, bh_ref, bl_ref, 0)
            odd = left_from(left_ref, bh_ref, bl_ref, 1)
            out_ref[k, 0] = even + odd
            out_ref[k, 1] = even - odd


def forward(pos, count, middle, ends, probe, lefts, rights):
    whole = pl.BlockSpec(memory_space=pltpu.VMEM)
    return pl.pallas_call(
        forward_kernel,
        out_shape=jax.ShapeDtypeStruct((TASKS, 2, PATCH, PATCH), f32),
        grid_spec=pltpu.PrefetchScalarGridSpec(
            num_scalar_prefetch=2,
            grid=(TASKS // 2,),
            in_specs=[pl.BlockSpec(memory_space=pl.ANY)] * 2 + [whole] * 3,
            out_specs=pl.BlockSpec((2, 2, PATCH, PATCH), lambda t, pos, count: (t, 0, 0, 0)),
            scratch_shapes=[pltpu.VMEM((2, 2, BLOCKS, 2, EXT // 2, HALF), f32), pltpu.SemaphoreType.DMA((3,))]
            + [pltpu.VMEM((2, PATCH, PATCH), bf16)] * 8,
        ),
        compiler_params=pltpu.CompilerParams(vmem_limit_bytes=40 << 20),
        cost_estimate=pl.CostEstimate(flops=TASKS * 24 * PATCH**3, bytes_accessed=TASKS * 8 * PATCH**2, transcendentals=0),
    )(pos, count, middle, ends, probe, lefts, rights)


def inverse_kernel(last, pos_ref, order_ref, slot_ref, count_ref, far_0, far_1, frame_0, frame_1, probe_ref, left_ref, right_ref, *rest):
    if last:
        perm_ref, before_ref = rest[:2]
        outs = rest[2:7]
        scratch = rest[7:15]
        acc_ref, even_ref, odd_ref, earlier_ref, sem = rest[15:]
        load = pltpu.make_async_copy(before_ref, earlier_ref, sem)
    else:
        acc_ref = rest[0]
        scratch = rest[1:]
    i = pl.program_id(0)

    @pl.when(i == 0)
    def _():
        if last:
            load.start()
        acc_ref[...] = jnp.zeros_like(acc_ref)

    @pl.when(2 * i < count_ref[0])
    def _():
        for k, far_ref, frame_ref in ((0, far_0, frame_0), (1, far_1, frame_1)):
            sh_ref, sl_ref = scratch[4 * k : 4 * k + 2]
            step = 32
            for at in range(0, HALF, step):
                parts = []
                for h in range(2):
                    re = far_ref[0, h, at : at + step, :]
                    im = far_ref[0, h, HALF + at : HALF + at + step, :]
                    weight = re * re + im * im - frame_ref[0, h * HALF + at : h * HALF + at + step, :]
                    parts.append((weight * re, weight * im))
                for c in range(2):
                    r = slice(c * HALF + at, c * HALF + at + step)
                    put(sh_ref, sl_ref, (0, r), parts[0][c] + parts[1][c])
                    put(sh_ref, sl_ref, (1, r), parts[0][c] - parts[1][c])
        for k in range(2):
            sh_ref, sl_ref, th_ref, tl_ref = scratch[4 * k : 4 * k + 4]
            for q in range(2):
                back = left_from(right_ref, sh_ref, sl_ref, q)
                r = slice(q * HALF, (q + 1) * HALF)
                for c in range(2):
                    lanes = slice(c * HALF, (c + 1) * HALF)
                    low, high = back[lanes, :HALF], back[lanes, HALF:]
                    put(th_ref, tl_ref, (0, r, lanes), low + high)
                    put(th_ref, tl_ref, (1, r, lanes), low - high)
        for k in range(2):
            th_ref, tl_ref = scratch[4 * k + 2 : 4 * k + 4]
            block, offset, rows = window(pos_ref, order_ref[2 * i + k])
            live = 2 * i + k < count_ref[0]
            for p in range(2):
                chi = right_from(th_ref, tl_ref, p, left_ref)
                mask = lane_mask(offset, p)
                for q in range(2):
                    parity, first = rows[q]
                    w = rolled_probe(probe_ref, offset, p, q)
                    r = slice(q * HALF, (q + 1) * HALF)
                    re, im = chi[r, :HALF], chi[r, HALF:]
                    g = [w[0] * re + w[1] * im, w[0] * im - w[1] * re]
                    for c in range(2):
                        here = acc_ref.at[c, p, block, parity, pl.ds(first, HALF), :]
                        there = acc_ref.at[c, p, block + 1, parity, pl.ds(first, HALF), :]
                        value = jnp.where(mask, here[...], there[...]) + g[c]
                        pltpu.store(here, value, mask=jnp.logical_and(mask, live))
                        pltpu.store(there, value, mask=jnp.logical_and(jnp.logical_not(mask), live))

    if last:

        @pl.when(i == pl.num_programs(0) - 1)
        def _():
            load.wait()
            for c in range(2):
                for b in range(BLOCKS):
                    for q in range(2):
                        even_ref[pl.ds(q, EXT // 2, stride=2), :] = acc_ref[c, 0, b, q] + earlier_ref[c, 0, b, q]
                        odd_ref[pl.ds(q, EXT // 2, stride=2), :] = acc_ref[c, 1, b, q] + earlier_ref[c, 1, b, q]
                    high, low = two_terms(jnp.concatenate([even_ref[...], odd_ref[...]], axis=1))
                    value = jnp.dot(high, perm_ref[...], preferred_element_type=f32)
                    value = value + jnp.dot(low, perm_ref[...], preferred_element_type=f32)
                    cols = slice(b * PATCH, (b + 1) * PATCH)
                    outs[3][c, :, cols] = value[:HALF]
                    outs[4][c, :, cols] = value[HALF + TILE :]
                    middle = value[HALF : HALF + TILE]
                    if b == 0:
                        outs[1][c] = middle[:, :HALF]
                        outs[0][c, :, :HALF] = middle[:, HALF:]
                    elif b == 1:
                        outs[0][c, :, HALF : HALF + PATCH] = middle
                    else:
                        outs[0][c, :, HALF + PATCH :] = middle[:, :HALF]
                        outs[2][c] = middle[:, HALF:]


def inverse(last, most, pos, order, slot, count, far, frames, probe, lefts, rights, before=None):
    whole = pl.BlockSpec(memory_space=pltpu.VMEM)
    parts = (2, 2, BLOCKS, 2, EXT // 2, HALF)
    more = (jnp.asarray(shuffle().T.copy()), before) if last else ()
    more_specs = [whole, pl.BlockSpec(memory_space=pl.ANY)] if last else []
    strips = [pltpu.VMEM(parts, f32)] + [pltpu.VMEM((EXT, HALF), f32)] * 2 + [pltpu.VMEM(parts, f32), pltpu.SemaphoreType.DMA]

    sizes = ((TILE, TILE), (TILE, HALF), (TILE, HALF), (HALF, EXT), (HALF, EXT))

    def far_spec(k):
        return pl.BlockSpec((1, 2, PATCH, PATCH), lambda i, pos, order, slot, count: (order[2 * i + k], 0, 0, 0))

    def frame_spec(k):
        return pl.BlockSpec((1, PATCH, PATCH), lambda i, pos, order, slot, count: (slot[2 * i + k], 0, 0))

    return pl.pallas_call(
        functools.partial(inverse_kernel, last),
        out_shape=[jax.ShapeDtypeStruct((2,) + size, f32) for size in sizes] if last else jax.ShapeDtypeStruct(parts, f32),
        grid_spec=pltpu.PrefetchScalarGridSpec(
            num_scalar_prefetch=4,
            grid=(most // 2,),
            in_specs=[far_spec(0), far_spec(1), frame_spec(0), frame_spec(1)] + [whole] * 3 + more_specs,
            out_specs=[whole] * 5 if last else whole,
            scratch_shapes=[pltpu.VMEM((2, PATCH, PATCH), bf16)] * 8 + (strips if last else []),
        ),
        compiler_params=pltpu.CompilerParams(vmem_limit_bytes=(40 if last else 44) << 20),
        cost_estimate=pl.CostEstimate(flops=most * 24 * PATCH**3, bytes_accessed=most * 12 * PATCH**2, transcendentals=0),
    )(pos, order, slot, count, far, far, frames, frames, probe, lefts, rights, *more)


def strips_kernel(object_ref, first_ref, last_ref, sem):
    size = object_ref.shape[2]
    copies = [
        pltpu.make_async_copy(object_ref.at[:, :, pl.ds(0, HALF)], first_ref, sem.at[0]),
        pltpu.make_async_copy(object_ref.at[:, :, pl.ds(size - HALF, HALF)], last_ref, sem.at[1]),
    ]
    for copy in copies:
        copy.start()
    for copy in copies:
        copy.wait()


def strips(block):
    strip = jax.ShapeDtypeStruct((2, block.shape[1], HALF), f32)
    return pl.pallas_call(
        strips_kernel,
        out_shape=(strip, strip),
        in_specs=[pl.BlockSpec(memory_space=pl.ANY)],
        out_specs=[pl.BlockSpec(memory_space=pltpu.VMEM)] * 2,
        scratch_shapes=[pltpu.SemaphoreType.DMA((2,))],
        compiler_params=pltpu.CompilerParams(vmem_limit_bytes=62 << 20),
        cost_estimate=pl.CostEstimate(flops=0, bytes_accessed=2 << 20, transcendentals=0),
    )(block)


def pick_kernel(slot, frames_ref, out_ref, buffer_ref, sem):
    count = sem.shape[1]
    size = out_ref.shape[0] // count
    pieces = [pl.ds(i * size, size) for i in range(count)]
    loads = [pltpu.make_async_copy(frames_ref.at[p, slot], buffer_ref.at[p], sem.at[0, i]) for i, p in enumerate(pieces)]
    stores = [pltpu.make_async_copy(buffer_ref.at[p], out_ref.at[p], sem.at[1, i]) for i, p in enumerate(pieces)]
    for load in loads:
        load.start()
    for load, store in zip(loads, stores):
        load.wait()
        store.start()
    for store in stores:
        store.wait()


def pick(kept, slot):
    shape = (kept.shape[0], PATCH, PATCH)
    return pl.pallas_call(
        functools.partial(pick_kernel, slot),
        out_shape=jax.ShapeDtypeStruct(shape, f32),
        in_specs=[pl.BlockSpec(memory_space=pl.ANY)],
        out_specs=pl.BlockSpec(memory_space=pl.ANY),
        scratch_shapes=[pltpu.VMEM(shape, f32), pltpu.SemaphoreType.DMA((2, 4))],
        compiler_params=pltpu.CompilerParams(vmem_limit_bytes=58 << 20),
        cost_estimate=pl.CostEstimate(flops=0, bytes_accessed=8 << 20, transcendentals=0),
    )(kept)


def from_tile(sent, dy, dx):
    high, wide = lax.axis_size("gy"), lax.axis_size("gx")
    if dy == 0:
        return lax.ppermute(sent, "gx", [(i + dx, i) for i in range(wide) if 0 <= i + dx < wide])
    return lax.ppermute(sent, "gy", [(i + dy, i) for i in range(high) if 0 <= i + dy < high])


def final_kernel(object_ref, total_ref, left_ref, right_ref, up_ref, down_ref, left_ends, right_ends, out_ref):
    out_ref[...] = (1.0 - step_size * ridge) * object_ref[...] - step_size * total_ref[...]
    top, bottom = slice(0, HALF), slice(TILE - HALF, TILE)
    for rows, ref, at in ((top, up_ref, 0), (bottom, down_ref, HALF)):
        out_ref[:, rows, :] = out_ref[:, rows, :] - step_size * ref[:, :, HALF : HALF + TILE]
        for lanes, ends in ((top, left_ends), (bottom, right_ends)):
            out_ref[:, rows, lanes] = out_ref[:, rows, lanes] - step_size * ends[:, at : at + HALF]
    out_ref[:, :, top] = out_ref[:, :, top] - step_size * left_ref[...]
    out_ref[:, :, bottom] = out_ref[:, :, bottom] - step_size * right_ref[...]


def final(block, *parts):
    return pl.pallas_call(
        final_kernel,
        out_shape=jax.ShapeDtypeStruct(block.shape, f32),
        in_specs=[pl.BlockSpec(memory_space=pltpu.VMEM)] * 8,
        out_specs=pl.BlockSpec(memory_space=pltpu.VMEM),
        compiler_params=pltpu.CompilerParams(vmem_limit_bytes=16 << 20),
        cost_estimate=pl.CostEstimate(flops=4 * block.size, bytes_accessed=16 * block.size, transcendentals=0),
    )(block, *parts)


def ordered(chosen, helper_cols, most):
    task_ids = jnp.arange(TASKS, dtype=jnp.int32)
    place = jnp.sum(jnp.logical_and(chosen[None, :], task_ids[None, :] < task_ids[:, None]), axis=1)
    spot = jnp.logical_and(chosen[None, :], place[None, :] == jnp.arange(most)[:, None])
    order = jnp.sum(jnp.where(spot, task_ids[None, :], 0), axis=1).astype(jnp.int32)
    slot = jnp.sum(jnp.where(spot, helper_cols[None, :], 0), axis=1).astype(jnp.int32)
    return order, slot, jnp.sum(chosen).astype(jnp.int32).reshape(1)


def local(pieces, probe, arrived_0, arrived_1, offsets, helper_cols, count):
    task_ids = jnp.arange(TASKS, dtype=jnp.int32)
    same = helper_cols[:, None] == helper_cols[None, :]
    second = jnp.any(jnp.logical_and(same, task_ids[None, :] < task_ids[:, None]), axis=1)
    valid = task_ids < count[0]
    order_0 = ordered(jnp.logical_and(valid, jnp.logical_not(second)), helper_cols, 16)
    order_1 = ordered(jnp.logical_and(valid, second), helper_cols, TASKS // 2)
    lefts, rights = tables()
    tile, left, right, up, down = pieces
    pro, middle = middle_rows(probe, tile, left, right)
    ends = end_rows(up, down)
    far = forward(offsets, count, middle, ends, pro, lefts, rights)
    part = inverse(False, 16, offsets, *order_0, far, arrived_0, pro, lefts, rights)
    return inverse(True, TASKS // 2, offsets, *order_1, far, arrived_1, pro, lefts, rights, part)


def per_device(object_field, probe, frames, positions, helpers, task_counts):
    first, last = strips(object_field)
    kept = frames[0, 0]
    left, right = from_tile(last, 0, -1), from_tile(first, 0, 1)
    arrived_0 = lax.all_to_all(pick(kept, 0), "gx", split_axis=0, concat_axis=0, tiled=True)
    again, _ = lax.optimization_barrier((kept, arrived_0))
    arrived_1 = lax.all_to_all(pick(again, 1), "gx", split_axis=0, concat_axis=0, tiled=True)
    above = jnp.concatenate([left[:, -HALF:], object_field[:, -HALF:], right[:, -HALF:]], axis=2)
    below = jnp.concatenate([left[:, :HALF], object_field[:, :HALF], right[:, :HALF]], axis=2)
    up, down = from_tile(above, -1, 0), from_tile(below, 1, 0)
    parts = local(
        [object_field, left, right, up, down],
        probe,
        arrived_0,
        arrived_1,
        positions[0, 0].reshape(-1),
        helpers[0, 0, :, 0],
        task_counts[0],
    )
    middle, to_left, to_right, to_up, to_down = parts
    up, down = from_tile(to_down, -1, 0), from_tile(to_up, 1, 0)
    left, right = from_tile(to_right, 0, -1), from_tile(to_left, 0, 1)
    first_ends = jnp.concatenate([up[:, :, :HALF], down[:, :, :HALF]], axis=1)
    last_ends = jnp.concatenate([up[:, :, -HALF:], down[:, :, -HALF:]], axis=1)
    left_ends, right_ends = from_tile(last_ends, 0, -1), from_tile(first_ends, 0, 1)
    return final(object_field, middle, left, right, up, down, left_ends, right_ends)


def solution(mesh):
    in_specs = (
        P(None, "gy", "gx"),
        P(),
        P("gy", "gx", None, None, None, None),
        P("gy", "gx", None, None),
        P("gy", "gx", None, None),
        P("gy", "gx"),
    )
    out_specs = P(None, "gy", "gx")
    return jax.shard_map(per_device, mesh=mesh, in_specs=in_specs, out_specs=out_specs, check_vma=False)
```

```python
import functools

import jax
import jax.numpy as jnp
import ml_dtypes
import numpy as np
from jax import lax
from jax.experimental import pallas as pl
from jax.experimental.pallas import tpu as pltpu
from jax.sharding import PartitionSpec as P


PATCH = 256
HALF = 128
TASKS = 24
TILE = 512
BLOCKS = 3
EXT = 768


step_size = 0.1
ridge = 0.5

f32 = jnp.float32
bf16 = jnp.bfloat16


def tables():
    j = np.arange(HALF)
    even = np.exp(-2j * np.pi * (np.outer(j, 2 * j) % PATCH) / PATCH) / 16.0
    odd = np.exp(-2j * np.pi * (np.outer(j, 2 * j + 1) % PATCH) / PATCH) / 16.0

    def left(w):
        return np.block([[w.real, -w.imag], [w.imag, w.real]])

    def split(w):
        high = w.astype(ml_dtypes.bfloat16)
        low = (w - high.astype(np.float64)).astype(ml_dtypes.bfloat16)
        return high, low

    pairs = [split(left(w)) for w in (even, odd)]
    lefts = np.stack([np.stack(pair) for pair in pairs])
    return jnp.asarray(lefts), jnp.asarray(np.swapaxes(lefts, 2, 3).copy())


def shuffle():
    p = np.zeros((PATCH, PATCH), np.float32)
    j = np.arange(HALF)
    p[2 * j, j] = 1
    p[2 * j + 1, HALF + j] = 1
    return p.astype(ml_dtypes.bfloat16)


def two_terms(x):
    high = x.astype(bf16)
    low = (x - high.astype(f32)).astype(bf16)
    return high, low


def three_dot(x, p):
    high = x.astype(bf16)
    rest = x - high.astype(f32)
    mid = rest.astype(bf16)
    low = (rest - mid.astype(f32)).astype(bf16)
    out = jnp.dot(high, p, preferred_element_type=f32)
    out = out + jnp.dot(mid, p, preferred_element_type=f32)
    return out + jnp.dot(low, p, preferred_element_type=f32)


def spread(value, perm_ref, out_ref, c, b, even_ref, odd_ref):
    rows = value.shape[0]
    mixed = three_dot(value, perm_ref[...])
    even_ref[:rows] = mixed[:, :HALF]
    odd_ref[:rows] = mixed[:, HALF:]
    for q in range(2):
        out_ref[c, 0, b, q] = even_ref[pl.ds(q, rows // 2, stride=2), :]
        out_ref[c, 1, b, q] = odd_ref[pl.ds(q, rows // 2, stride=2), :]


def middle_kernel(probe_ref, tile_ref, left_ref, right_ref, perm_ref, probe_out, out_ref, even_ref, odd_ref):
    size = tile_ref.shape[2]
    for c in range(2):
        spread(probe_ref[c], perm_ref, probe_out, c, 0, even_ref, odd_ref)
        for b in range(BLOCKS):
            if b == 0:
                value = jnp.concatenate([left_ref[c], tile_ref[c, :, :HALF]], axis=1)
            elif b == 1:
                value = tile_ref[c, :, HALF : size - HALF]
            else:
                value = jnp.concatenate([tile_ref[c, :, size - HALF :], right_ref[c]], axis=1)
            spread(value, perm_ref, out_ref, c, b, even_ref, odd_ref)


def middle_rows(probe, tile, left, right):
    whole = pl.BlockSpec(memory_space=pltpu.VMEM)
    return pl.pallas_call(
        middle_kernel,
        out_shape=(
            jax.ShapeDtypeStruct((2, 2, 1, 2, HALF, HALF), f32),
            jax.ShapeDtypeStruct((2, 2, BLOCKS, 2, TILE // 2, HALF), f32),
        ),
        in_specs=[whole] * 5,
        out_specs=[whole] * 2,
        scratch_shapes=[pltpu.VMEM((TILE, HALF), f32)] * 2,
        compiler_params=pltpu.CompilerParams(vmem_limit_bytes=30 << 20),
        cost_estimate=pl.CostEstimate(flops=6 * TILE * EXT * PATCH * 2, bytes_accessed=16 * TILE * EXT, transcendentals=0),
    )(probe, tile, left, right, jnp.asarray(shuffle()))


def ends_kernel(up_ref, down_ref, perm_ref, out_ref, even_ref, odd_ref):
    for side, ref in enumerate((up_ref, down_ref)):
        for c in range(2):
            for b in range(BLOCKS):
                spread(ref[c, :, b * PATCH : (b + 1) * PATCH], perm_ref, out_ref.at[side], c, b, even_ref, odd_ref)


def end_rows(up, down):
    whole = pl.BlockSpec(memory_space=pltpu.VMEM)
    return pl.pallas_call(
        ends_kernel,
        out_shape=jax.ShapeDtypeStruct((2, 2, 2, BLOCKS, 2, HALF // 2, HALF), f32),
        in_specs=[whole] * 3,
        out_specs=whole,
        scratch_shapes=[pltpu.VMEM((HALF, HALF), f32)] * 2,
        compiler_params=pltpu.CompilerParams(vmem_limit_bytes=30 << 20),
        cost_estimate=pl.CostEstimate(flops=6 * PATCH * EXT * PATCH * 2, bytes_accessed=16 * PATCH * EXT, transcendentals=0),
    )(up, down, jnp.asarray(shuffle()))


def window(pos_ref, t):
    start_y = pos_ref[2 * t] + HALF
    start_x = pos_ref[2 * t + 1] + HALF
    block = jnp.where(start_x >= PATCH, 1, 0)
    offset = start_x - block * PATCH
    rows = [((start_y + q) & 1, (start_y + q) >> 1) for q in range(2)]
    return block, offset, rows


def rolled_probe(probe_ref, offset, p, q):
    source = (p + offset) & 1
    amount = ((offset + source - p) >> 1) & (HALF - 1)
    return [pltpu.roll(probe_ref[c, source, 0, q], amount, 1) for c in range(2)]


def lane_mask(offset, p):
    lane = lax.broadcasted_iota(jnp.int32, (HALF, HALF), 1)
    return lane >= ((offset + 1 - p) >> 1)


def put(high_ref, low_ref, where, value):
    high, low = two_terms(value)
    high_ref[where] = high
    low_ref[where] = low


def right_from(high_ref, low_ref, k, w_ref):
    high = high_ref[k]
    w = w_ref[k, 0]
    out = jnp.dot(
        jnp.concatenate([high, low_ref[k], high], axis=1),
        jnp.concatenate([w, w, w_ref[k, 1]], axis=0),
        preferred_element_type=f32,
    )
    return out


def left_from(w_ref, high_ref, low_ref, k):
    high = high_ref[k]
    w = w_ref[k, 0]
    return jnp.dot(
        jnp.concatenate([w, w, w_ref[k, 1]], axis=1),
        jnp.concatenate([high, low_ref[k], high], axis=0),
        preferred_element_type=f32,
    )


def forward_kernel(pos_ref, count_ref, middle_ref, ends_ref, probe_ref, left_ref, right_ref, out_ref, obj_ref, sem, *scratch):
    step = pl.program_id(0)

    @pl.when(step == 0)
    def _():
        end = HALF // 2
        spans = ((ends_ref.at[0], 0, end), (middle_ref, end, TILE // 2), (ends_ref.at[1], end + TILE // 2, end))
        copies = [
            pltpu.make_async_copy(source, obj_ref.at[:, :, :, :, pl.ds(first, size), :], sem.at[k])
            for k, (source, first, size) in enumerate(spans)
        ]
        for copy in copies:
            copy.start()
        for copy in copies:
            copy.wait()

    @pl.when(2 * step < count_ref[0])
    def _():
        for k in range(2):
            ah_ref, al_ref = scratch[4 * k : 4 * k + 2]
            block, offset, rows = window(pos_ref, 2 * step + k)
            for p in range(2):
                mask = lane_mask(offset, p)
                for q in range(2):
                    parity, first = rows[q]
                    o = [
                        jnp.where(
                            mask,
                            obj_ref[c, p, block, parity, pl.ds(first, HALF), :],
                            obj_ref[c, p, block + 1, parity, pl.ds(first, HALF), :],
                        )
                        for c in range(2)
                    ]
                    w = rolled_probe(probe_ref, offset, p, q)
                    r = slice(q * HALF, (q + 1) * HALF)
                    put(ah_ref, al_ref, (p, r, slice(0, HALF)), w[0] * o[0] - w[1] * o[1])
                    put(ah_ref, al_ref, (p, r, slice(HALF, PATCH)), w[0] * o[1] + w[1] * o[0])
        for k in range(2):
            ah_ref, al_ref, bh_ref, bl_ref = scratch[4 * k : 4 * k + 4]
            even = right_from(ah_ref, al_ref, 0, right_ref)
            odd = right_from(ah_ref, al_ref, 1, right_ref)
            for q in range(2):
                r = slice(q * HALF, (q + 1) * HALF)
                for c in range(2):
                    lanes = slice(c * HALF, (c + 1) * HALF)
                    put(bh_ref, bl_ref, (q, lanes, slice(0, HALF)), even[r, lanes] + odd[r, lanes])
                    put(bh_ref, bl_ref, (q, lanes, slice(HALF, PATCH)), even[r, lanes] - odd[r, lanes])
        for k in range(2):
            bh_ref, bl_ref = scratch[4 * k + 2 : 4 * k + 4]
            even = left_from(left_ref, bh_ref, bl_ref, 0)
            odd = left_from(left_ref, bh_ref, bl_ref, 1)
            out_ref[k, 0] = even + odd
            out_ref[k, 1] = even - odd


def forward(pos, count, middle, ends, probe, lefts, rights):
    whole = pl.BlockSpec(memory_space=pltpu.VMEM)
    return pl.pallas_call(
        forward_kernel,
        out_shape=jax.ShapeDtypeStruct((TASKS, 2, PATCH, PATCH), f32),
        grid_spec=pltpu.PrefetchScalarGridSpec(
            num_scalar_prefetch=2,
            grid=(TASKS // 2,),
            in_specs=[pl.BlockSpec(memory_space=pl.ANY)] * 2 + [whole] * 3,
            out_specs=pl.BlockSpec((2, 2, PATCH, PATCH), lambda t, pos, count: (t, 0, 0, 0)),
            scratch_shapes=[pltpu.VMEM((2, 2, BLOCKS, 2, EXT // 2, HALF), f32), pltpu.SemaphoreType.DMA((3,))]
            + [pltpu.VMEM((2, PATCH, PATCH), bf16)] * 8,
        ),
        compiler_params=pltpu.CompilerParams(vmem_limit_bytes=40 << 20),
        cost_estimate=pl.CostEstimate(flops=TASKS * 24 * PATCH**3, bytes_accessed=TASKS * 8 * PATCH**2, transcendentals=0),
    )(pos, count, middle, ends, probe, lefts, rights)


def inverse_kernel(last, pos_ref, order_ref, slot_ref, count_ref, far_0, far_1, frame_0, frame_1, probe_ref, left_ref, right_ref, *rest):
    if last:
        perm_ref, before_ref = rest[:2]
        outs = rest[2:7]
        scratch = rest[7:15]
        acc_ref, even_ref, odd_ref, earlier_ref, sem = rest[15:]
        load = pltpu.make_async_copy(before_ref, earlier_ref, sem)
    else:
        acc_ref, probe_out = rest[:2]
        scratch = rest[2:]
    i = pl.program_id(0)

    @pl.when(i == 0)
    def _():
        if last:
            load.start()
        else:
            probe_out[...] = probe_ref[...]
        acc_ref[...] = jnp.zeros_like(acc_ref)

    @pl.when(2 * i < count_ref[0])
    def _():
        for k, far_ref, frame_ref in ((0, far_0, frame_0), (1, far_1, frame_1)):
            sh_ref, sl_ref = scratch[4 * k : 4 * k + 2]
            step = 32
            for at in range(0, HALF, step):
                parts = []
                for h in range(2):
                    re = far_ref[0, h, at : at + step, :]
                    im = far_ref[0, h, HALF + at : HALF + at + step, :]
                    weight = re * re + im * im - frame_ref[0, h * HALF + at : h * HALF + at + step, :]
                    parts.append((weight * re, weight * im))
                for c in range(2):
                    r = slice(c * HALF + at, c * HALF + at + step)
                    put(sh_ref, sl_ref, (0, r), parts[0][c] + parts[1][c])
                    put(sh_ref, sl_ref, (1, r), parts[0][c] - parts[1][c])
        for k in range(2):
            sh_ref, sl_ref, th_ref, tl_ref = scratch[4 * k : 4 * k + 4]
            for q in range(2):
                back = left_from(right_ref, sh_ref, sl_ref, q)
                r = slice(q * HALF, (q + 1) * HALF)
                for c in range(2):
                    lanes = slice(c * HALF, (c + 1) * HALF)
                    low, high = back[lanes, :HALF], back[lanes, HALF:]
                    put(th_ref, tl_ref, (0, r, lanes), low + high)
                    put(th_ref, tl_ref, (1, r, lanes), low - high)
        for k in range(2):
            th_ref, tl_ref = scratch[4 * k + 2 : 4 * k + 4]
            block, offset, rows = window(pos_ref, order_ref[2 * i + k])
            live = 2 * i + k < count_ref[0]
            for p in range(2):
                chi = right_from(th_ref, tl_ref, p, left_ref)
                mask = lane_mask(offset, p)
                for q in range(2):
                    parity, first = rows[q]
                    w = rolled_probe(probe_ref, offset, p, q)
                    r = slice(q * HALF, (q + 1) * HALF)
                    re, im = chi[r, :HALF], chi[r, HALF:]
                    g = [w[0] * re + w[1] * im, w[0] * im - w[1] * re]
                    for c in range(2):
                        here = acc_ref.at[c, p, block, parity, pl.ds(first, HALF), :]
                        there = acc_ref.at[c, p, block + 1, parity, pl.ds(first, HALF), :]
                        value = jnp.where(mask, here[...], there[...]) + g[c]
                        pltpu.store(here, value, mask=jnp.logical_and(mask, live))
                        pltpu.store(there, value, mask=jnp.logical_and(jnp.logical_not(mask), live))

    if last:

        @pl.when(i == pl.num_programs(0) - 1)
        def _():
            load.wait()
            for c in range(2):
                for b in range(BLOCKS):
                    for q in range(2):
                        even_ref[pl.ds(q, EXT // 2, stride=2), :] = acc_ref[c, 0, b, q] + earlier_ref[c, 0, b, q]
                        odd_ref[pl.ds(q, EXT // 2, stride=2), :] = acc_ref[c, 1, b, q] + earlier_ref[c, 1, b, q]
                    high, low = two_terms(jnp.concatenate([even_ref[...], odd_ref[...]], axis=1))
                    value = jnp.dot(high, perm_ref[...], preferred_element_type=f32)
                    value = value + jnp.dot(low, perm_ref[...], preferred_element_type=f32)
                    cols = slice(b * PATCH, (b + 1) * PATCH)
                    outs[3][c, :, cols] = value[:HALF]
                    outs[4][c, :, cols] = value[HALF + TILE :]
                    middle = value[HALF : HALF + TILE]
                    if b == 0:
                        outs[1][c] = middle[:, :HALF]
                        outs[0][c, :, :HALF] = middle[:, HALF:]
                    elif b == 1:
                        outs[0][c, :, HALF : HALF + PATCH] = middle
                    else:
                        outs[0][c, :, HALF + PATCH :] = middle[:, :HALF]
                        outs[2][c] = middle[:, HALF:]


def inverse(last, most, pos, order, slot, count, far, frames, probe, lefts, rights, before=None):
    whole = pl.BlockSpec(memory_space=pltpu.VMEM)
    parts = (2, 2, BLOCKS, 2, EXT // 2, HALF)
    more = (jnp.asarray(shuffle().T.copy()), before) if last else ()
    more_specs = [whole, pl.BlockSpec(memory_space=pl.ANY)] if last else []
    strips = [pltpu.VMEM(parts, f32)] + [pltpu.VMEM((EXT, HALF), f32)] * 2 + [pltpu.VMEM(parts, f32), pltpu.SemaphoreType.DMA]

    sizes = ((TILE, TILE), (TILE, HALF), (TILE, HALF), (HALF, EXT), (HALF, EXT))

    def far_spec(k):
        return pl.BlockSpec((1, 2, PATCH, PATCH), lambda i, pos, order, slot, count: (order[2 * i + k], 0, 0, 0))

    def frame_spec(k):
        return pl.BlockSpec((1, PATCH, PATCH), lambda i, pos, order, slot, count: (slot[2 * i + k], 0, 0))

    return pl.pallas_call(
        functools.partial(inverse_kernel, last),
        out_shape=[jax.ShapeDtypeStruct((2,) + size, f32) for size in sizes]
        if last
        else [jax.ShapeDtypeStruct(parts, f32), jax.ShapeDtypeStruct(probe.shape, f32)],
        grid_spec=pltpu.PrefetchScalarGridSpec(
            num_scalar_prefetch=4,
            grid=(most // 2,),
            in_specs=[far_spec(0), far_spec(1), frame_spec(0), frame_spec(1)] + [whole] * 3 + more_specs,
            out_specs=[whole] * (5 if last else 2),
            scratch_shapes=[pltpu.VMEM((2, PATCH, PATCH), bf16)] * 8 + (strips if last else []),
        ),
        compiler_params=pltpu.CompilerParams(vmem_limit_bytes=(40 if last else 44) << 20),
        cost_estimate=pl.CostEstimate(flops=most * 24 * PATCH**3, bytes_accessed=most * 12 * PATCH**2, transcendentals=0),
    )(pos, order, slot, count, far, far, frames, frames, probe, lefts, rights, *more)


def strips_kernel(object_ref, first_ref, last_ref, sem):
    size = object_ref.shape[2]
    copies = [
        pltpu.make_async_copy(object_ref.at[:, :, pl.ds(0, HALF)], first_ref, sem.at[0]),
        pltpu.make_async_copy(object_ref.at[:, :, pl.ds(size - HALF, HALF)], last_ref, sem.at[1]),
    ]
    for copy in copies:
        copy.start()
    for copy in copies:
        copy.wait()


def strips(block):
    strip = jax.ShapeDtypeStruct((2, block.shape[1], HALF), f32)
    return pl.pallas_call(
        strips_kernel,
        out_shape=(strip, strip),
        in_specs=[pl.BlockSpec(memory_space=pl.ANY)],
        out_specs=[pl.BlockSpec(memory_space=pltpu.VMEM)] * 2,
        scratch_shapes=[pltpu.SemaphoreType.DMA((2,))],
        compiler_params=pltpu.CompilerParams(vmem_limit_bytes=62 << 20),
        cost_estimate=pl.CostEstimate(flops=0, bytes_accessed=2 << 20, transcendentals=0),
    )(block)


def pick_kernel(slot, frames_ref, out_ref, buffer_ref, sem):
    count = sem.shape[1]
    size = out_ref.shape[0] // count
    pieces = [pl.ds(i * size, size) for i in range(count)]
    loads = [pltpu.make_async_copy(frames_ref.at[p, slot], buffer_ref.at[p], sem.at[0, i]) for i, p in enumerate(pieces)]
    stores = [pltpu.make_async_copy(buffer_ref.at[p], out_ref.at[p], sem.at[1, i]) for i, p in enumerate(pieces)]
    for load in loads:
        load.start()
    for load, store in zip(loads, stores):
        load.wait()
        store.start()
    for store in stores:
        store.wait()


def pick(kept, slot):
    shape = (kept.shape[0], PATCH, PATCH)
    return pl.pallas_call(
        functools.partial(pick_kernel, slot),
        out_shape=jax.ShapeDtypeStruct(shape, f32),
        in_specs=[pl.BlockSpec(memory_space=pl.ANY)],
        out_specs=pl.BlockSpec(memory_space=pl.ANY),
        scratch_shapes=[pltpu.VMEM(shape, f32), pltpu.SemaphoreType.DMA((2, 4))],
        compiler_params=pltpu.CompilerParams(vmem_limit_bytes=58 << 20),
        cost_estimate=pl.CostEstimate(flops=0, bytes_accessed=8 << 20, transcendentals=0),
    )(kept)


def from_tile(sent, dy, dx):
    high, wide = lax.axis_size("gy"), lax.axis_size("gx")
    if dy == 0:
        return lax.ppermute(sent, "gx", [(i + dx, i) for i in range(wide) if 0 <= i + dx < wide])
    return lax.ppermute(sent, "gy", [(i + dy, i) for i in range(high) if 0 <= i + dy < high])


def final_kernel(object_ref, total_ref, left_ref, right_ref, up_ref, down_ref, left_ends, right_ends, out_ref):
    out_ref[...] = (1.0 - step_size * ridge) * object_ref[...] - step_size * total_ref[...]
    top, bottom = slice(0, HALF), slice(TILE - HALF, TILE)
    for rows, ref, at in ((top, up_ref, 0), (bottom, down_ref, HALF)):
        out_ref[:, rows, :] = out_ref[:, rows, :] - step_size * ref[:, :, HALF : HALF + TILE]
        for lanes, ends in ((top, left_ends), (bottom, right_ends)):
            out_ref[:, rows, lanes] = out_ref[:, rows, lanes] - step_size * ends[:, at : at + HALF]
    out_ref[:, :, top] = out_ref[:, :, top] - step_size * left_ref[...]
    out_ref[:, :, bottom] = out_ref[:, :, bottom] - step_size * right_ref[...]


def final(block, *parts):
    return pl.pallas_call(
        final_kernel,
        out_shape=jax.ShapeDtypeStruct(block.shape, f32),
        in_specs=[pl.BlockSpec(memory_space=pltpu.VMEM)] * 8,
        out_specs=pl.BlockSpec(memory_space=pltpu.VMEM),
        compiler_params=pltpu.CompilerParams(vmem_limit_bytes=16 << 20),
        cost_estimate=pl.CostEstimate(flops=4 * block.size, bytes_accessed=16 * block.size, transcendentals=0),
    )(block, *parts)


def ordered(chosen, helper_cols, most):
    task_ids = jnp.arange(TASKS, dtype=jnp.int32)
    place = jnp.sum(jnp.logical_and(chosen[None, :], task_ids[None, :] < task_ids[:, None]), axis=1)
    spot = jnp.logical_and(chosen[None, :], place[None, :] == jnp.arange(most)[:, None])
    order = jnp.sum(jnp.where(spot, task_ids[None, :], 0), axis=1).astype(jnp.int32)
    slot = jnp.sum(jnp.where(spot, helper_cols[None, :], 0), axis=1).astype(jnp.int32)
    return order, slot, jnp.sum(chosen).astype(jnp.int32).reshape(1)


def local(pieces, probe, arrived_0, arrived_1, offsets, helper_cols, count):
    task_ids = jnp.arange(TASKS, dtype=jnp.int32)
    same = helper_cols[:, None] == helper_cols[None, :]
    second = jnp.any(jnp.logical_and(same, task_ids[None, :] < task_ids[:, None]), axis=1)
    valid = task_ids < count[0]
    order_0 = ordered(jnp.logical_and(valid, jnp.logical_not(second)), helper_cols, 16)
    order_1 = ordered(jnp.logical_and(valid, second), helper_cols, TASKS // 2)
    lefts, rights = tables()
    tile, left, right, up, down = pieces
    pro, middle = middle_rows(probe, tile, left, right)
    ends = end_rows(up, down)
    far = forward(offsets, count, middle, ends, pro, lefts, rights)
    part, pro = inverse(False, 16, offsets, *order_0, far, arrived_0, pro, lefts, rights)
    return inverse(True, TASKS // 2, offsets, *order_1, far, arrived_1, pro, lefts, rights, part)


def per_device(object_field, probe, frames, positions, helpers, task_counts):
    first, last = strips(object_field)
    kept = frames[0, 0]
    left, right = from_tile(last, 0, -1), from_tile(first, 0, 1)
    arrived_0 = lax.all_to_all(pick(kept, 0), "gx", split_axis=0, concat_axis=0, tiled=True)
    again, _ = lax.optimization_barrier((kept, arrived_0))
    arrived_1 = lax.all_to_all(pick(again, 1), "gx", split_axis=0, concat_axis=0, tiled=True)
    above = jnp.concatenate([left[:, -HALF:], object_field[:, -HALF:], right[:, -HALF:]], axis=2)
    below = jnp.concatenate([left[:, :HALF], object_field[:, :HALF], right[:, :HALF]], axis=2)
    up, down = from_tile(above, -1, 0), from_tile(below, 1, 0)
    parts = local(
        [object_field, left, right, up, down],
        probe,
        arrived_0,
        arrived_1,
        positions[0, 0].reshape(-1),
        helpers[0, 0, :, 0],
        task_counts[0],
    )
    middle, to_left, to_right, to_up, to_down = parts
    up, down = from_tile(to_down, -1, 0), from_tile(to_up, 1, 0)
    left, right = from_tile(to_right, 0, -1), from_tile(to_left, 0, 1)
    first_ends = jnp.concatenate([up[:, :, :HALF], down[:, :, :HALF]], axis=1)
    last_ends = jnp.concatenate([up[:, :, -HALF:], down[:, :, -HALF:]], axis=1)
    left_ends, right_ends = from_tile(last_ends, 0, -1), from_tile(first_ends, 0, 1)
    return final(object_field, middle, left, right, up, down, left_ends, right_ends)


def solution(mesh):
    in_specs = (
        P(None, "gy", "gx"),
        P(),
        P("gy", "gx", None, None, None, None),
        P("gy", "gx", None, None),
        P("gy", "gx", None, None),
        P("gy", "gx"),
    )
    out_specs = P(None, "gy", "gx")
    return jax.shard_map(per_device, mesh=mesh, in_specs=in_specs, out_specs=out_specs, check_vma=False)
```
